32 devices in a mesh: groups: 2 (over y), rows: 16 (over z, x, core).
Axes of the slice: x: 2, y: 2, z: 4, core: 2. Of those that a mesh axis runs over, the one named last changes fastest.
Arguments:
- response_tiles: bfloat16 [128, 30, 128, 128], P(('groups', 'rows')), parts along dimension 0, may hold values from -0.09375 to 0.09375
- tile_cols: int32 [128, 30], P(('groups', 'rows')), parts along dimension 0, may hold values from 0 to 63, as said below
- tile_count: int32 [128], P(('groups', 'rows')), parts along dimension 0, may hold values from 15 to 30
- heat_start: float32 [16384, 128], P(('groups', 'rows')), parts along dimension 0, may hold values from -6 to 6
- recorded_well_warmth: float32 [1024, 128], P(('groups', 'rows')), parts along dimension 0, may hold values from -18 to 18
- bore_lengths: int32 [32, 32], P(('groups', 'rows')), parts along dimension 0, may hold values from 1 to 24, 512 in all within a row
Outputs:
- heat_rates: float32 [16384, 128], P(('groups', 'rows')), parts along dimension 0
- bore_misfit: float32 [1024, 128], P(('groups', 'rows')), parts along dimension 0
The draws below stay inside these ranges and needn't reach their ends.
There are 2 independent parts, one for each index of `groups`. The reference program is written for one: setup_inputs(seed, part) draws one part's arguments, and reference() takes and returns one part's arrays. A program takes and returns all parts, laid end to end along the dimension named above; each array names one. Nothing has to cross between parts.
Inputs may be any that keep to these rules, and one draw needn't show every extreme that they name: `tile_cols`: for block row i the first tile_count[i] entries are distinct block columns c with |c - i| <= 16; the other entries equal i and are unused.
All inputs are finite; a program needn't handle non-finite values.
Results may differ from the reference program's by a relative error of at most 0.0046.
Values may be sent and summed in bfloat16 or wider, within the bound.
No kernel may reach another device: no remote copies, remote signals or barrier semaphores. Data moves between devices by JAX's collectives and lax.ppermute only.
A program may use at most 64 MiB of HBM per device.

```python
import math
import jax
import jax.numpy as jnp
import numpy as np
from jax import lax

TILE = 128
W = 128
BR = 4
K = 30
ITERS = 2
MOST_SEG = 24
BH_DEV = 32
SPAN = 16
ROWS_DEV = 512
RANKS = 16
NBR = 64
SEG = 8192
BORE = 512


def tile_lists(key):
    key_perm, key_count = jax.random.split(jax.random.fold_in(key, 11))
    band_width = 2 * SPAN + 1
    shuffled = jax.vmap(lambda sub_key: jax.random.permutation(sub_key, band_width))(jax.random.split(key_perm, NBR))
    block_index = jnp.arange(NBR, dtype=jnp.int32)[:, None]
    candidate = block_index + shuffled.astype(jnp.int32) - SPAN
    usable = (candidate >= 0) & (candidate < NBR)
    ranking = jnp.where(usable, 0, band_width) + jnp.arange(band_width, dtype=jnp.int32)[None, :]
    ranked_order = jnp.argsort(ranking, axis=1)
    picked = jnp.take_along_axis(candidate, ranked_order, axis=1)[:, :K]
    available = jnp.sum(usable.astype(jnp.int32), axis=1)
    wanted = jax.random.randint(key_count, (NBR,), K // 2, K + 1).astype(jnp.int32)
    wanted = wanted.at[NBR // 2].set(K)
    in_count = jnp.minimum(wanted, available).astype(jnp.int32)
    slot_index = jnp.arange(K, dtype=jnp.int32)[None, :]
    columns = jnp.where(slot_index < in_count[:, None], picked, block_index)
    return (columns.astype(jnp.int32), in_count)


def draw_tile_cols(key, part):
    return tile_lists(key)[0]


def draw_tile_count(key, part):
    return tile_lists(key)[1]


def draw_recorded_well_warmth(key, part):
    row_ramp = 1.0 + 2.0 * jnp.arange(BORE, dtype=jnp.float32)[:, None] / (BORE - 1)
    values = jnp.clip(jax.random.normal(key, (BORE, W), dtype=jnp.float32), -6.0, 6.0)
    return (values * row_ramp).astype(jnp.float32)


def level_of(rng, dims, shards, low, high):
    gain = 1.0
    for dim, parts in shards:
        draws = jax.random.uniform(jax.random.fold_in(jax.random.fold_in(rng, 6), dim), (parts,), jnp.float32, low / len(shards), high / len(shards))
        gain = gain * jnp.repeat(jnp.exp(draws), dims[dim] // parts).reshape((-1,) + (1,) * (len(dims) - 1 - dim))
    return gain


def length_profile(count, total, limit, skew):
    portions = [(1 << 20) // math.isqrt(standing ** skew) + 1 for standing in range(2, count + 1)]
    spare, given = total - limit - (count - 1), [1] * (count - 1)
    while spare > 0:
        candidates = [i for i in range(count - 1) if given[i] < limit]
        whole, left = sum([portions[i] for i in candidates]), spare
        for i in candidates:
            more = min(limit - given[i], max(1, left * portions[i] // whole), spare)
            given[i] = given[i] + more
            spare = spare - more
    return np.array([limit] + given)


def ragged(rng, amount, total, most, skew):
    if amount == 2:
        one = jax.random.randint(rng, (), max(1, total - most), min(most, total - 1) + 1)
        return jnp.stack([one, total - one])
    tallies = jnp.asarray(length_profile(amount, total, most, skew), jnp.int32)
    pairs = (amount - 1) // 2
    donor, receiver = tallies[1:1 + 2 * pairs:2], tallies[2:2 + 2 * pairs:2]
    slack = jnp.minimum(donor - 1, most - receiver)
    moved = jax.random.randint(jax.random.fold_in(rng, 1), (pairs,), 0, 1 << 20) % (slack + 1)
    tallies = tallies.at[1:1 + 2 * pairs:2].set(donor - moved).at[2:2 + 2 * pairs:2].set(receiver + moved)
    return tallies[jax.random.permutation(jax.random.fold_in(rng, 2), amount)]


def normal_values(rng, extent, deviation, most, cuts=(), held_as=jnp.bfloat16):
    values = jax.random.normal(rng, extent, jnp.float32) * deviation
    if len(cuts) > 0:
        values = level_of(rng, extent, cuts, -0.22, 0.18) * values
    return jnp.clip(values, min=-most, max=most).astype(held_as)


def setup_inputs(seed: int = 0, part: int = 0) -> dict:
    streams_of = jax.random.split(jax.random.key(seed), 7)
    part_splits = jax.random.split(jax.random.fold_in(streams_of[6], part), 7)
    return {
        "response_tiles": normal_values(part_splits[0], (NBR, K, TILE, TILE), (K * TILE) ** -0.5, 0.09375, ((0, 16),)),
        "tile_cols": draw_tile_cols(jax.random.fold_in(jax.random.fold_in(streams_of[6], part), 71), part),
        "tile_count": draw_tile_count(jax.random.fold_in(jax.random.fold_in(streams_of[6], part), 71), part),
        "heat_start": normal_values(part_splits[3], (SEG, W), 1.0, 6.0, ((0, 16),), jnp.float32),
        "recorded_well_warmth": draw_recorded_well_warmth(jax.random.fold_in(jax.random.fold_in(streams_of[6], part), 71), part),
        "bore_lengths": jax.vmap(lambda own: ragged(own, BH_DEV, ROWS_DEV, MOST_SEG, 0))(jax.random.split(part_splits[5], RANKS)).reshape((RANKS, BH_DEV)).astype(jnp.int32),
    }


def bore_members(lengths, seg_rows):
    bore_ends = jnp.cumsum(lengths).astype(jnp.int32)
    starts = bore_ends - lengths
    position = jnp.arange(seg_rows, dtype=jnp.int32)
    inside = (position[None, :] >= starts[:, None]) & (position[None, :] < bore_ends[:, None])
    return inside.astype(jnp.float32)


def quantized_entries(values):
    return lax.optimization_barrier(values.astype(jnp.bfloat16)).astype(jnp.float32)


def reference(response_tiles, tile_cols, tile_count, heat_start, recorded_well_warmth, bore_lengths):
    in_use = jnp.arange(K, dtype=jnp.int32)[None, :] < tile_count[:, None]
    tiles_ranked = response_tiles.reshape(RANKS, BR, K, TILE, TILE)
    cols_ranked = tile_cols.reshape(RANKS, BR, K)
    use_ranked = in_use.reshape(RANKS, BR, K)
    members = jax.vmap(lambda lengths: bore_members(lengths, ROWS_DEV))(bore_lengths)
    counts = bore_lengths.astype(jnp.float32)

    def predicted_output(field):
        blocks = field.reshape(NBR, TILE, W)

        def one_rank(inputs):
            tiles_here, cols_here, used_here = inputs
            panels = jnp.where(used_here[:, :, None, None], blocks[cols_here], 0.0)
            return jnp.einsum("bkij,bkjt->bit", tiles_here.astype(jnp.float32), panels,
                              precision=lax.Precision.HIGHEST)

        return lax.map(one_rank, (tiles_ranked, cols_ranked, use_ranked)).reshape(SEG, W)

    def adjoint(residual):
        blocks = residual.reshape(RANKS, BR, TILE, W)

        def one_rank(summed, inputs):
            tiles_here, cols_here, used_here, resid_here = inputs
            products = jnp.einsum("bkij,bit->bkjt", tiles_here.astype(jnp.float32), resid_here,
                                  precision=lax.Precision.HIGHEST)
            products = jnp.where(used_here[:, :, None, None], products, 0.0)
            summed = summed.at[cols_here.reshape(-1)].add(products.reshape(BR * K, TILE, W))
            return summed, None

        summed, unused_out = lax.scan(one_rank, jnp.zeros((NBR, TILE, W), jnp.float32),
                                      (tiles_ranked, cols_ranked, use_ranked, blocks))
        return summed.reshape(SEG, W)

    def well_mean_warmth(field):
        sums = jnp.einsum("rbs,rst->rbt", members, field.reshape(RANKS, ROWS_DEV, W),
                          precision=lax.Precision.HIGHEST)
        return (sums / counts[:, :, None]).reshape(BORE, W)

    def spread(squared_error_total):
        shares = squared_error_total.reshape(RANKS, BH_DEV, W) / counts[:, :, None]
        return jnp.einsum("rbs,rbt->rst", members, shares, precision=lax.Precision.HIGHEST).reshape(SEG, W)

    source_power_entries = heat_start
    thermal_profile = predicted_output(quantized_entries(source_power_entries))
    for iteration in range(ITERS):
        squared_error_total = well_mean_warmth(thermal_profile) - recorded_well_warmth
        segment_residual = quantized_entries(spread(squared_error_total))
        gradient = adjoint(segment_residual)
        operator_product_entries = predicted_output(quantized_entries(gradient))
        image_mean = well_mean_warmth(operator_product_entries)
        descent_stride = jnp.sum(gradient * gradient) / (jnp.sum(image_mean * image_mean) + 1e-6)
        source_power_entries = source_power_entries - descent_stride * gradient
        thermal_profile = thermal_profile - descent_stride * operator_product_entries
    return source_power_entries, well_mean_warmth(thermal_profile) - recorded_well_warmth
```

```python
import functools

import jax
import jax.numpy as jnp
from jax import lax
from jax.experimental import pallas as pl
from jax.experimental.pallas import tpu as pltpu
from jax.sharding import PartitionSpec as P

REACH = 4
ITERS = 2
CHIP_REACH = REACH // 2
WINDOW = 2 * CHIP_REACH + 1
F32 = jnp.float32
BF16 = jnp.bfloat16
VMEM = pl.BlockSpec(memory_space=pltpu.VMEM)
SMEM = pl.BlockSpec(memory_space=pltpu.SMEM)
ANY = pl.BlockSpec(memory_space=pl.ANY)


def hop_offsets(chip):
    near = 1 - 2 * lax.rem(chip, 2)
    far = 2 - 4 * lax.rem(chip // 2, 2)
    return (near, -near, far, -far)


def hop_pairs(ranks):
    chips = ranks // 2
    groups = []
    for step in (1, 2):
        for phase in (0, 1):
            pairs = []
            for chip in range(chips - step):
                if (chip // step) % 2 == phase:
                    for core in (0, 1):
                        low, high = 2 * chip + core, 2 * (chip + step) + core
                        pairs += [(low, high), (high, low)]
            groups.append(pairs)
    return groups


def bounds(lengths, bores):
    upto = lax.broadcasted_iota(jnp.int32, (bores, bores), 1) <= lax.broadcasted_iota(
        jnp.int32, (bores, bores), 0
    )
    ends = jnp.sum(jnp.where(upto, lengths.astype(F32), 0.0), axis=1, keepdims=True)
    here = lax.broadcasted_iota(jnp.int32, (bores, bores), 1) == lax.broadcasted_iota(
        jnp.int32, (bores, bores), 0
    )
    counts = jnp.sum(jnp.where(here, lengths.astype(F32), 0.0), axis=1, keepdims=True)
    return ends, counts


def compress_kernel(me_ref, cols_ref, count_ref, lengths_ref, tiles_hbm, *rest):
    outs = rest[: WINDOW]
    slab, tiles, sems = rest[WINDOW:]
    block_rows, slots, tile = tiles.shape[0], tiles.shape[1], tiles.shape[2]
    bores = slab.shape[1]
    per_chip = 2 * block_rows
    half = slots // 2
    copies = []
    for row in range(block_rows):
        for part in range(2):
            where = pl.ds(part * half, half)
            copy = pltpu.make_async_copy(
                tiles_hbm.at[row, where], tiles.at[row, where], sems.at[row, part]
            )
            copy.start()
            copies.append(copy)
    chip = me_ref[0] // 2
    first_block = (chip - CHIP_REACH) * per_chip
    ends, counts = bounds(lengths_ref[...], bores)
    starts = ends - counts
    slab[...] = jnp.zeros_like(slab)
    for row in range(block_rows):
        position = (
            lax.broadcasted_iota(jnp.int32, (bores, tile), 1) + row * tile
        ).astype(F32)
        members = ((position >= starts) & (position < ends)).astype(F32).astype(BF16)
        used = count_ref[row]
        for part in range(2):
            copies[2 * row + part].wait()
            for slot in range(part * half, part * half + half):
                place = jnp.where(
                    slot < used, cols_ref[row, slot] - first_block, WINDOW * per_chip
                )
                slab[place] += jnp.dot(
                    members, tiles[row, slot], preferred_element_type=F32
                )
    for out, offset in zip(outs, (0,) + hop_offsets(chip)):
        out[...] = slab[pl.ds((offset + CHIP_REACH) * per_chip, per_chip)]


def split(value):
    high = value.astype(BF16)
    return high, (value - high.astype(F32)).astype(BF16)


def gram_kernel(me_ref, *rest):
    mine, other = rest[:WINDOW], rest[WINDOW : 2 * WINDOW]
    heat_mine, heat_other = rest[2 * WINDOW : 2 * WINDOW + 2]
    outs = rest[2 * WINDOW + 2 : 3 * WINDOW + 2]
    high, low, heat, left, shifted = rest[3 * WINDOW + 2 :]
    blocks, bores, tile = mine[0].shape
    chip, core = me_ref[0] // 2, lax.rem(me_ref[0], 2)
    seg_rows = heat_mine.shape[0]
    offsets = (0,) + hop_offsets(chip)
    for pieces, side in ((mine, core), (other, 1 - core)):
        for piece, offset in zip(pieces, offsets):
            at = pl.multiple_of((offset + CHIP_REACH) * 2 * bores + side * bores, bores)
            for block in range(blocks):
                top, rest_of = split(piece[block])
                high[pl.ds(at, bores), block * tile : (block + 1) * tile] = top
                low[pl.ds(at, bores), block * tile : (block + 1) * tile] = rest_of
    heat[pl.ds(pl.multiple_of(core * seg_rows, seg_rows), seg_rows)] = heat_mine[...]
    heat[pl.ds(pl.multiple_of((1 - core) * seg_rows, seg_rows), seg_rows)] = heat_other[...]
    for slot in range(WINDOW):
        at = pl.multiple_of(slot * 2 * bores + core * bores, bores)
        left[slot * bores : (slot + 1) * bores] = high[pl.ds(at, bores)]
        left[(WINDOW + slot) * bores : (WINDOW + slot + 1) * bores] = low[pl.ds(at, bores)]
    rows = WINDOW * bores
    transposed = (((1,), (1,)), ((), ()))
    both = lax.dot_general(left[...], high[...], transposed, preferred_element_type=F32)
    cross = lax.dot_general(left[:rows], low[...], transposed, preferred_element_type=F32)
    gram = both[:rows] + both[rows:] + cross
    warm = jnp.dot(left[...], heat[...], preferred_element_type=F32)
    warm = warm[:rows] + warm[rows:]
    span = 2 * bores
    width = 3 * 2 * span
    lane = lax.broadcasted_iota(jnp.int32, (bores, width), 1)
    padded = jnp.concatenate(
        [gram, jnp.zeros((rows, width - WINDOW * span), F32)], axis=1
    )
    for slot in range(WINDOW):
        offset = slot - CHIP_REACH
        base = padded[slot * bores : (slot + 1) * bores]
        odd = lax.rem(chip + offset + 2, 2)
        places = []
        for parity in (0, 1):
            shift = (CHIP_REACH - offset + parity) * span
            moved = pltpu.roll(base, shift % width, 1) if shift % width else base
            keep = (lane >= shift) & (lane < (WINDOW + parity) * span)
            places.append(jnp.where(keep, moved, 0.0))
        shifted[slot, :, :width] = jnp.where(odd == 1, places[1], places[0])
        shifted[slot, :, width:] = warm[slot * bores : (slot + 1) * bores]
    for out, offset in zip(outs, offsets):
        out[...] = shifted[offset + CHIP_REACH]


def total_kernel(me_ref, lengths_ref, recorded_ref, *rest):
    parts, out = rest[:WINDOW], rest[WINDOW]
    bores, columns = recorded_ref.shape
    width = out.shape[1] - columns
    span = 2 * bores
    odd = lax.rem(me_ref[0] // 2, 2)
    _, counts = bounds(lengths_ref[...], bores)
    total = parts[0][...]
    for part in parts[1:]:
        total = total + part[...]
    lane = lax.broadcasted_iota(jnp.int32, (bores, width), 1)
    free = ((odd == 1) & (lane < span)) | ((odd == 0) & (lane >= WINDOW * span))
    out[:, :width] = jnp.where(free, counts, total[:, :width])
    out[:, width:] = total[:, width:] / counts - recorded_ref[...]


def transpose_kernel(me_ref, *rest):
    mine, other = rest[:WINDOW], rest[WINDOW : 2 * WINDOW]
    high, low = rest[2 * WINDOW : 2 * WINDOW + 2]
    (rows_of,) = rest[2 * WINDOW + 2 :]
    blocks, bores, tile = mine[0].shape
    own_blocks = blocks // 2
    chip, core = me_ref[0] // 2, lax.rem(me_ref[0], 2)
    for pieces, side in ((mine, core), (other, 1 - core)):
        for piece, offset in zip(pieces, (0,) + hop_offsets(chip)):
            at = pl.multiple_of((offset + CHIP_REACH) * 2 * bores + side * bores, bores)
            for block in range(own_blocks):
                rows_of[block, pl.ds(at, bores)] = piece[core * own_blocks + block]
    for block in range(own_blocks):
        top, rest_of = split(rows_of[block].T)
        high[block * tile : (block + 1) * tile] = top
        low[block * tile : (block + 1) * tile] = rest_of


def descend_kernel(ranks, me_ref, heat_ref, high_ref, low_ref, *rest):
    pieces = rest[:ranks]
    heat_out, misfit_out = rest[ranks : ranks + 2]
    lower, band, counts, misfit, warm, shares = rest[ranks + 2 :]
    bores, columns = misfit_out.shape
    width = lower.shape[1]
    plane = 4 * bores
    planes = ranks // 4
    span = 2 * bores
    me = me_ref[0]
    lane = lax.broadcasted_iota(jnp.int32, (bores, width), 1)
    for index, piece in enumerate(pieces):
        rank = jnp.bitwise_xor(me, index)
        at = pl.multiple_of(rank * bores, bores)
        odd = lax.rem(rank // 2, 2) == 1
        count = jnp.where(odd, piece[:, :1], piece[:, width - 1 : width])
        free = (odd & (lane < span)) | (jnp.logical_not(odd) & (lane >= WINDOW * span))
        lower[pl.ds(at, bores)] = jnp.where(free, 0.0, piece[:, :width])
        misfit[pl.ds(at, bores)] = piece[:, width:]
        counts[pl.ds(at, bores)] = jnp.broadcast_to(count, (bores, columns))
    half_row = lax.broadcasted_iota(jnp.int32, (plane, plane), 0) < span
    half_col = lax.broadcasted_iota(jnp.int32, (plane, plane), 1) >= span
    for p in range(planes):
        rows = lower[p * plane : (p + 1) * plane]
        diagonal = rows[:, 2 * plane :]
        diagonal = jnp.where(half_row & half_col, diagonal.T, diagonal)
        after = []
        for step in (1, 2):
            if p + step < planes:
                following = lower[(p + step) * plane : (p + step + 1) * plane]
                after.append(following[:, (2 - step) * plane : (3 - step) * plane].T)
            else:
                after.append(jnp.zeros((plane, plane), F32))
        whole = [rows[:, :plane], rows[:, plane : 2 * plane], diagonal] + after
        for index, part in enumerate(whole):
            top, rest_of = split(part)
            band[p, :plane, index * plane : (index + 1) * plane] = top
            band[p, plane:, index * plane : (index + 1) * plane] = rest_of
    shares[:, : 2 * plane] = jnp.zeros((ITERS, 2 * plane, columns), BF16)
    shares[:, (planes + 2) * plane :] = jnp.zeros((ITERS, 2 * plane, columns), BF16)
    steps = []
    for iteration in range(ITERS):
        shares[iteration, 2 * plane : (planes + 2) * plane] = (
            misfit[...] / counts[...]
        ).astype(BF16)
        power = jnp.zeros((plane, columns), F32)
        curvature = jnp.zeros((plane, columns), F32)
        for p in range(planes):
            both = jnp.dot(
                band[p],
                shares[iteration, p * plane : (p + 5) * plane],
                preferred_element_type=F32,
            )
            swept = both[:plane] + both[plane:]
            here = shares[iteration, (p + 2) * plane : (p + 3) * plane].astype(F32)
            image = swept / counts[p * plane : (p + 1) * plane]
            warm[p * plane : (p + 1) * plane] = image
            power = power + here * swept
            curvature = curvature + image * image
        step = jnp.sum(power) / (jnp.sum(curvature) + 1e-06)
        steps.append(step)
        misfit[...] = misfit[...] - step * warm[...]
    misfit_out[...] = misfit[pl.ds(pl.multiple_of(me * bores, bores), bores)]
    first = pl.multiple_of((me // 2 - CHIP_REACH) * span + 2 * plane, span)
    heat = heat_ref[...]
    for iteration in range(ITERS):
        near = shares[iteration, pl.ds(first, WINDOW * span)]
        gradient = jnp.dot(high_ref[...], near, preferred_element_type=F32) + jnp.dot(
            low_ref[...], near, preferred_element_type=F32
        )
        heat = heat - steps[iteration] * gradient
    heat_out[...] = heat


def on_device(
    ranks, response_tiles, tile_cols, tile_count, heat_start, recorded, bore_lengths
):
    block_rows, slots, tile = response_tiles.shape[:3]
    seg_rows, columns = heat_start.shape
    bores = bore_lengths.shape[1]
    per_chip = 2 * block_rows
    rows = WINDOW * bores
    span = 2 * bores
    width = 6 * span
    me = lax.axis_index("rows").astype(jnp.int32).reshape(1)
    hops = hop_pairs(ranks)
    limit = pltpu.CompilerParams(vmem_limit_bytes=48 << 20)

    def send(value, pairs):
        return lax.ppermute(value, "rows", pairs)

    def swap(value, bit):
        return send(value, [(rank, rank ^ bit) for rank in range(ranks)])

    heat_low = heat_start.astype(BF16)
    heat_other = swap(heat_low, 1)
    piece = jax.ShapeDtypeStruct((per_chip, bores, tile), F32)
    sent = pl.pallas_call(
        compress_kernel,
        out_shape=(piece,) * WINDOW,
        in_specs=[SMEM, SMEM, SMEM, VMEM, ANY],
        out_specs=(VMEM,) * WINDOW,
        scratch_shapes=[
            pltpu.VMEM((WINDOW * per_chip + 1, bores, tile), F32),
            pltpu.VMEM((block_rows, slots, tile, tile), BF16),
            pltpu.SemaphoreType.DMA((block_rows, 2)),
        ],
        compiler_params=limit,
        name="compress",
    )(me, tile_cols, tile_count, bore_lengths, response_tiles)
    mine = [sent[0]] + [send(value, pairs) for value, pairs in zip(sent[1:], hops)]
    other = [swap(value, 1) for value in mine]
    packed = jax.ShapeDtypeStruct((bores, width + columns), F32)
    partial = pl.pallas_call(
        gram_kernel,
        out_shape=(packed,) * WINDOW,
        in_specs=[SMEM] + [VMEM] * (2 * WINDOW + 2),
        out_specs=(VMEM,) * WINDOW,
        scratch_shapes=[
            pltpu.VMEM((WINDOW * span, per_chip * tile), BF16),
            pltpu.VMEM((WINDOW * span, per_chip * tile), BF16),
            pltpu.VMEM((2 * seg_rows, columns), BF16),
            pltpu.VMEM((2 * rows, per_chip * tile), BF16),
            pltpu.VMEM((WINDOW, bores, width + columns), F32),
        ],
        compiler_params=limit,
        name="gram",
    )(me, *mine, *other, heat_low, heat_other)
    parts = [partial[0]] + [send(value, pairs) for value, pairs in zip(partial[1:], hops)]
    turned = jax.ShapeDtypeStruct((seg_rows, WINDOW * span), BF16)
    high, low = pl.pallas_call(
        transpose_kernel,
        out_shape=(turned, turned),
        in_specs=[SMEM] + [VMEM] * (2 * WINDOW),
        out_specs=(VMEM, VMEM),
        scratch_shapes=[pltpu.VMEM((block_rows, WINDOW * span, tile), F32)],
        compiler_params=limit,
        name="turn",
    )(me, *mine, *other)
    total = pl.pallas_call(
        total_kernel,
        out_shape=packed,
        in_specs=[SMEM] + [VMEM] * (2 + WINDOW),
        out_specs=VMEM,
        name="total",
    )(me, bore_lengths, recorded, *parts)
    gathered = [total] + [None] * (ranks - 1)
    known = [0]
    direct = [index for index in range(4, min(ranks, 16), 4)]
    for index in direct:
        gathered[index] = swap(total, index)
    known += direct
    bit = 16
    order = []
    while bit < ranks:
        order.append(bit)
        bit *= 2
    for bit in order + [2, 1]:
        for index in list(known):
            gathered[index ^ bit] = swap(gathered[index], bit)
            known.append(index ^ bit)
    return pl.pallas_call(
        functools.partial(descend_kernel, ranks),
        out_shape=(
            jax.ShapeDtypeStruct((seg_rows, columns), F32),
            jax.ShapeDtypeStruct((bores, columns), F32),
        ),
        in_specs=[SMEM] + [VMEM] * (3 + ranks),
        out_specs=(VMEM, VMEM),
        scratch_shapes=[
            pltpu.VMEM((ranks * bores, width), F32),
            pltpu.VMEM((ranks // 4, 8 * bores, 20 * bores), BF16),
            pltpu.VMEM((ranks * bores, columns), F32),
            pltpu.VMEM((ranks * bores, columns), F32),
            pltpu.VMEM((ranks * bores, columns), F32),
            pltpu.VMEM((ITERS, (ranks + 16) * bores, columns), BF16),
        ],
        compiler_params=limit,
        name="descend",
    )(me, heat_start, high, low, *gathered)


def solution(mesh):
    placed = (
        P(("groups", "rows"), None, None, None),
        P(("groups", "rows"), None),
        P(("groups", "rows")),
        P(("groups", "rows"), None),
        P(("groups", "rows"), None),
        P(("groups", "rows"), None),
    )
    return jax.shard_map(
        functools.partial(on_device, mesh.shape["rows"]),
        mesh=mesh,
        in_specs=placed,
        out_specs=(P(("groups", "rows"), None), P(("groups", "rows"), None)),
        check_vma=False,
    )
```

```python
import functools

import jax
import jax.numpy as jnp
from jax import lax
from jax.experimental import pallas as pl
from jax.experimental.pallas import tpu as pltpu
from jax.sharding import PartitionSpec as P

REACH = 4
ITERS = 2
CHIP_REACH = REACH // 2
WINDOW = 2 * CHIP_REACH + 1
F32 = jnp.float32
BF16 = jnp.bfloat16
VMEM = pl.BlockSpec(memory_space=pltpu.VMEM)
HBM = pl.BlockSpec(memory_space=pltpu.HBM)


def hop_offsets(chip):
    near = 1 - 2 * lax.rem(chip, 2)
    far = 2 - 4 * lax.rem(chip // 2, 2)
    return (-near, -far, far, near)


def hop_pairs(ranks):
    chips = ranks // 2
    groups = []
    for step, phase in ((1, 1), (2, 1), (2, 0), (1, 0)):
        pairs = []
        for chip in range(chips - step):
            if (chip // step) % 2 == phase:
                for core in (0, 1):
                    low, high = 2 * chip + core, 2 * (chip + step) + core
                    pairs += [(low, high), (high, low)]
        groups.append(pairs)
    return groups


def bounds(lengths, bores):
    upto = lax.broadcasted_iota(jnp.int32, (bores, bores), 1) <= lax.broadcasted_iota(
        jnp.int32, (bores, bores), 0
    )
    ends = jnp.sum(jnp.where(upto, lengths.astype(F32), 0.0), axis=1, keepdims=True)
    here = lax.broadcasted_iota(jnp.int32, (bores, bores), 1) == lax.broadcasted_iota(
        jnp.int32, (bores, bores), 0
    )
    counts = jnp.sum(jnp.where(here, lengths.astype(F32), 0.0), axis=1, keepdims=True)
    return ends, counts


def compress_kernel(cols_hbm, count_hbm, lengths_hbm, tiles_hbm, *rest):
    outs = rest[: WINDOW]
    cols_ref, count_ref, lengths_ref, slab, tiles, small_sems, sems = rest[WINDOW:]
    small = []
    for index, (source, target) in enumerate(
        ((cols_hbm, cols_ref), (count_hbm, count_ref), (lengths_hbm, lengths_ref))
    ):
        copy = pltpu.make_async_copy(source, target, small_sems.at[index])
        copy.start()
        small.append(copy)
    block_rows, slots, tile = tiles.shape[0], tiles.shape[1], tiles.shape[2]
    bores = slab.shape[1]
    per_chip = 2 * block_rows
    copies = []
    for row in range(block_rows):
        copy = pltpu.make_async_copy(tiles_hbm.at[row], tiles.at[row], sems.at[row])
        copy.start()
        copies.append(copy)
    slab[...] = jnp.zeros_like(slab)
    chip = lax.axis_index("rows") // 2
    for copy in small:
        copy.wait()
    first_block = (chip - CHIP_REACH) * per_chip
    ends, counts = bounds(lengths_ref[...], bores)
    starts = ends - counts
    members = []
    for row in range(block_rows):
        position = (
            lax.broadcasted_iota(jnp.int32, (bores, tile), 1) + row * tile
        ).astype(F32)
        inside = (position >= starts) & (position < ends)
        members.append(inside.astype(F32).astype(BF16))
    empty = jnp.zeros((bores, tile), BF16)
    for row in range(0, block_rows, 2):
        upper = jnp.concatenate([members[row], empty], axis=1)
        under = jnp.concatenate([empty, members[row + 1]], axis=1)
        left = jnp.concatenate([upper, under], axis=0)
        copies[row].wait()
        copies[row + 1].wait()
        for slot in range(0, slots, 2):
            right = jnp.concatenate(
                [
                    jnp.concatenate([tiles[at, slot], tiles[at, slot + 1]], axis=1)
                    for at in (row, row + 1)
                ],
                axis=0,
            )
            product = jnp.dot(left, right, preferred_element_type=F32)
            for i in range(2):
                for j in range(2):
                    place = jnp.where(
                        slot + j < count_ref[row + i],
                        cols_ref[row + i, slot + j] - first_block,
                        WINDOW * per_chip,
                    )
                    slab[place] += product[
                        i * bores : (i + 1) * bores, j * tile : (j + 1) * tile
                    ]
    for out, offset in zip(outs, (0,) + hop_offsets(chip)):
        out[...] = slab[pl.ds((offset + CHIP_REACH) * per_chip, per_chip)]


def split(value):
    high = value.astype(BF16)
    return high, (value - high.astype(F32)).astype(BF16)


def gram_kernel(lengths_ref, recorded_ref, *rest):
    mine, other = rest[:WINDOW], rest[WINDOW : 2 * WINDOW]
    heat_mine, heat_other = rest[2 * WINDOW : 2 * WINDOW + 2]
    outs = rest[2 * WINDOW + 2 : 3 * WINDOW + 2]
    high, low, heat, left, shifted = rest[3 * WINDOW + 2 :]
    blocks, bores, tile = mine[0].shape
    me = lax.axis_index("rows")
    chip, core = me // 2, lax.rem(me, 2)
    seg_rows = heat_mine.shape[0]
    offsets = (0,) + hop_offsets(chip)
    for pieces, side in ((mine, core), (other, 1 - core)):
        for piece, offset in zip(pieces, offsets):
            at = pl.multiple_of((offset + CHIP_REACH) * 2 * bores + side * bores, bores)
            for block in range(blocks):
                top, rest_of = split(piece[block])
                high[pl.ds(at, bores), block * tile : (block + 1) * tile] = top
                low[pl.ds(at, bores), block * tile : (block + 1) * tile] = rest_of
    heat[pl.ds(pl.multiple_of(core * seg_rows, seg_rows), seg_rows)] = heat_mine[...]
    heat[pl.ds(pl.multiple_of((1 - core) * seg_rows, seg_rows), seg_rows)] = heat_other[...]
    for slot in range(WINDOW):
        at = pl.multiple_of(slot * 2 * bores + core * bores, bores)
        left[slot * bores : (slot + 1) * bores] = high[pl.ds(at, bores)]
        left[(WINDOW + slot) * bores : (WINDOW + slot + 1) * bores] = low[pl.ds(at, bores)]
    rows = WINDOW * bores
    transposed = (((1,), (1,)), ((), ()))
    both = lax.dot_general(left[...], high[...], transposed, preferred_element_type=F32)
    cross = lax.dot_general(left[:rows], low[...], transposed, preferred_element_type=F32)
    gram = both[:rows] + both[rows:] + cross
    warm = jnp.dot(left[...], heat[...], preferred_element_type=F32)
    warm = warm[:rows] + warm[rows:]
    span = 2 * bores
    width = 3 * 2 * span
    lane = lax.broadcasted_iota(jnp.int32, (bores, width), 1)
    padded = jnp.concatenate(
        [gram, jnp.zeros((rows, width - WINDOW * span), F32)], axis=1
    )
    for slot in range(WINDOW):
        offset = slot - CHIP_REACH
        base = padded[slot * bores : (slot + 1) * bores]
        odd = lax.rem(chip + offset + 2, 2)
        places = []
        for parity in (0, 1):
            shift = (CHIP_REACH - offset + parity) * span
            moved = pltpu.roll(base, shift % width, 1) if shift % width else base
            keep = (lane >= shift) & (lane < (WINDOW + parity) * span)
            places.append(jnp.where(keep, moved, 0.0))
        shifted[slot, :, :width] = jnp.where(odd == 1, places[1], places[0])
        shifted[slot, :, width:] = warm[slot * bores : (slot + 1) * bores]
    _, counts = bounds(lengths_ref[...], bores)
    odd = lax.rem(chip, 2)
    free = ((odd == 1) & (lane < span)) | ((odd == 0) & (lane >= WINDOW * span))
    shifted[CHIP_REACH, :, :width] = jnp.where(
        free, counts, shifted[CHIP_REACH, :, :width]
    )
    shifted[CHIP_REACH, :, width:] = (
        shifted[CHIP_REACH, :, width:] - counts * recorded_ref[...]
    )
    for out, offset in zip(outs, offsets):
        out[...] = shifted[offset + CHIP_REACH]


def transpose_kernel(*rest):
    mine, other = rest[:WINDOW], rest[WINDOW : 2 * WINDOW]
    high, low = rest[2 * WINDOW : 2 * WINDOW + 2]
    (rows_of,) = rest[2 * WINDOW + 2 :]
    blocks, bores, tile = mine[0].shape
    own_blocks = blocks // 2
    me = lax.axis_index("rows")
    chip, core = me // 2, lax.rem(me, 2)
    for pieces, side in ((mine, core), (other, 1 - core)):
        for piece, offset in zip(pieces, (0,) + hop_offsets(chip)):
            at = pl.multiple_of((offset + CHIP_REACH) * 2 * bores + side * bores, bores)
            for block in range(own_blocks):
                rows_of[block, pl.ds(at, bores)] = piece[core * own_blocks + block]
    for block in range(own_blocks):
        top, rest_of = split(rows_of[block].T)
        high[block * tile : (block + 1) * tile] = top
        low[block * tile : (block + 1) * tile] = rest_of


def descend_kernel(ranks, heat_hbm, high_ref, low_ref, *rest):
    pieces = rest[:ranks]
    heat_out, misfit_out = rest[ranks : ranks + 2]
    lower, band, counts, misfit, warm, shares, heat_ref, heat_sem = rest[ranks + 2 :]
    fetch = pltpu.make_async_copy(heat_hbm, heat_ref, heat_sem)
    fetch.start()
    bores, columns = misfit_out.shape
    width = lower.shape[1]
    plane = 4 * bores
    planes = ranks // 4
    span = 2 * bores
    me = lax.axis_index("rows")
    lane = lax.broadcasted_iota(jnp.int32, (bores, width), 1)
    for index, piece in enumerate(pieces):
        rank = jnp.bitwise_xor(me, index)
        at = pl.multiple_of(rank * bores, bores)
        odd = lax.rem(rank // 2, 2) == 1
        count = jnp.where(odd, piece[:, :1], piece[:, width - 1 : width])
        free = (odd & (lane < span)) | (jnp.logical_not(odd) & (lane >= WINDOW * span))
        lower[pl.ds(at, bores)] = jnp.where(free, 0.0, piece[:, :width])
        misfit[pl.ds(at, bores)] = piece[:, width:] / count
        counts[pl.ds(at, bores)] = jnp.broadcast_to(count, (bores, columns))
    half_row = lax.broadcasted_iota(jnp.int32, (plane, plane), 0) < span
    half_col = lax.broadcasted_iota(jnp.int32, (plane, plane), 1) >= span
    for p in range(planes):
        rows = lower[p * plane : (p + 1) * plane]
        diagonal = rows[:, 2 * plane :]
        diagonal = jnp.where(half_row & half_col, diagonal.T, diagonal)
        after = []
        for step in (1, 2):
            if p + step < planes:
                following = lower[(p + step) * plane : (p + step + 1) * plane]
                after.append(following[:, (2 - step) * plane : (3 - step) * plane].T)
            else:
                after.append(jnp.zeros((plane, plane), F32))
        whole = [rows[:, :plane], rows[:, plane : 2 * plane], diagonal] + after
        for index, part in enumerate(whole):
            top, rest_of = split(part)
            band[p, :plane, index * plane : (index + 1) * plane] = top
            band[p, plane:, index * plane : (index + 1) * plane] = rest_of
    shares[:, : 2 * plane] = jnp.zeros((ITERS, 2 * plane, columns), BF16)
    shares[:, (planes + 2) * plane :] = jnp.zeros((ITERS, 2 * plane, columns), BF16)
    steps = []
    for iteration in range(ITERS):
        shares[iteration, 2 * plane : (planes + 2) * plane] = (
            misfit[...] / counts[...]
        ).astype(BF16)
        power = jnp.zeros((plane, columns), F32)
        curvature = jnp.zeros((plane, columns), F32)
        for p in range(planes):
            both = jnp.dot(
                band[p],
                shares[iteration, p * plane : (p + 5) * plane],
                preferred_element_type=F32,
            )
            swept = both[:plane] + both[plane:]
            here = shares[iteration, (p + 2) * plane : (p + 3) * plane].astype(F32)
            image = swept / counts[p * plane : (p + 1) * plane]
            warm[p * plane : (p + 1) * plane] = image
            power = power + here * swept
            curvature = curvature + image * image
        step = jnp.sum(power) / (jnp.sum(curvature) + 1e-06)
        steps.append(step)
        misfit[...] = misfit[...] - step * warm[...]
    misfit_out[...] = misfit[pl.ds(pl.multiple_of(me * bores, bores), bores)]
    first = pl.multiple_of((me // 2 - CHIP_REACH) * span + 2 * plane, span)
    fetch.wait()
    heat = heat_ref[...]
    for iteration in range(ITERS):
        near = shares[iteration, pl.ds(first, WINDOW * span)]
        gradient = jnp.dot(high_ref[...], near, preferred_element_type=F32) + jnp.dot(
            low_ref[...], near, preferred_element_type=F32
        )
        heat = heat - steps[iteration] * gradient
    heat_out[...] = heat


def on_device(
    ranks, response_tiles, tile_cols, tile_count, heat_start, recorded, bore_lengths
):
    block_rows, slots, tile = response_tiles.shape[:3]
    seg_rows, columns = heat_start.shape
    bores = bore_lengths.shape[1]
    per_chip = 2 * block_rows
    rows = WINDOW * bores
    span = 2 * bores
    width = 6 * span
    hops = hop_pairs(ranks)
    limit = pltpu.CompilerParams(vmem_limit_bytes=48 << 20)

    def send(value, pairs):
        return lax.ppermute(value, "rows", pairs)

    def swap(value, bit):
        return send(value, [(rank, rank ^ bit) for rank in range(ranks)])

    heat_low = heat_start.astype(BF16)
    heat_other = swap(heat_low, 1)
    piece = jax.ShapeDtypeStruct((per_chip, bores, tile), F32)
    sent = pl.pallas_call(
        compress_kernel,
        out_shape=(piece,) * WINDOW,
        in_specs=[HBM] * 4,
        out_specs=(VMEM,) * WINDOW,
        scratch_shapes=[
            pltpu.SMEM(tile_cols.shape, jnp.int32),
            pltpu.SMEM(tile_count.shape, jnp.int32),
            pltpu.VMEM(bore_lengths.shape, jnp.int32),
            pltpu.VMEM((WINDOW * per_chip + 1, bores, tile), F32),
            pltpu.VMEM((block_rows, slots, tile, tile), BF16),
            pltpu.SemaphoreType.DMA((3,)),
            pltpu.SemaphoreType.DMA((block_rows,)),
        ],
        compiler_params=pltpu.CompilerParams(vmem_limit_bytes=60 << 20),
        name="compress",
    )(tile_cols, tile_count, bore_lengths, response_tiles)
    mine = [sent[0]] + [send(value, pairs) for value, pairs in zip(sent[1:], hops)]
    other = [swap(value, 1) for value in mine]
    packed = jax.ShapeDtypeStruct((bores, width + columns), F32)
    partial = pl.pallas_call(
        gram_kernel,
        out_shape=(packed,) * WINDOW,
        in_specs=[VMEM] * (2 * WINDOW + 4),
        out_specs=(VMEM,) * WINDOW,
        scratch_shapes=[
            pltpu.VMEM((WINDOW * span, per_chip * tile), BF16),
            pltpu.VMEM((WINDOW * span, per_chip * tile), BF16),
            pltpu.VMEM((2 * seg_rows, columns), BF16),
            pltpu.VMEM((2 * rows, per_chip * tile), BF16),
            pltpu.VMEM((WINDOW, bores, width + columns), F32),
        ],
        compiler_params=limit,
        name="gram",
    )(bore_lengths, recorded, *mine, *other, heat_low, heat_other)
    parts = [partial[0]] + [send(value, pairs) for value, pairs in zip(partial[1:], hops)]
    turned = jax.ShapeDtypeStruct((seg_rows, WINDOW * span), BF16)
    high, low = pl.pallas_call(
        transpose_kernel,
        out_shape=(turned, turned),
        in_specs=[VMEM] * (2 * WINDOW),
        out_specs=(VMEM, VMEM),
        scratch_shapes=[pltpu.VMEM((block_rows, WINDOW * span, tile), F32)],
        compiler_params=limit,
        name="turn",
    )(*mine, *other)
    total = parts[0]
    for part in parts[1:]:
        total = total + part
    gathered = [total] + [None] * (ranks - 1)
    known = [0]
    direct = [index for index in range(4, min(ranks, 16), 4)][::-1]
    for index in direct:
        gathered[index] = swap(total, index)
    known += direct
    bit = 16
    order = []
    while bit < ranks:
        order.append(bit)
        bit *= 2
    for bit in order + [2, 1]:
        for index in list(known):
            gathered[index ^ bit] = swap(gathered[index], bit)
            known.append(index ^ bit)
    return pl.pallas_call(
        functools.partial(descend_kernel, ranks),
        out_shape=(
            jax.ShapeDtypeStruct((seg_rows, columns), F32),
            jax.ShapeDtypeStruct((bores, columns), F32),
        ),
        in_specs=[HBM] + [VMEM] * (2 + ranks),
        out_specs=(VMEM, VMEM),
        scratch_shapes=[
            pltpu.VMEM((ranks * bores, width), F32),
            pltpu.VMEM((ranks // 4, 8 * bores, 20 * bores), BF16),
            pltpu.VMEM((ranks * bores, columns), F32),
            pltpu.VMEM((ranks * bores, columns), F32),
            pltpu.VMEM((ranks * bores, columns), F32),
            pltpu.VMEM((ITERS, (ranks + 16) * bores, columns), BF16),
            pltpu.VMEM((seg_rows, columns), F32),
            pltpu.SemaphoreType.DMA,
        ],
        compiler_params=limit,
        name="descend",
    )(heat_start, high, low, *gathered)


def solution(mesh):
    placed = (
        P(("groups", "rows"), None, None, None),
        P(("groups", "rows"), None),
        P(("groups", "rows")),
        P(("groups", "rows"), None),
        P(("groups", "rows"), None),
        P(("groups", "rows"), None),
    )
    return jax.shard_map(
        functools.partial(on_device, mesh.shape["rows"]),
        mesh=mesh,
        in_specs=placed,
        out_specs=(P(("groups", "rows"), None), P(("groups", "rows"), None)),
        check_vma=False,
    )
```

```python
import functools

import jax
import jax.numpy as jnp
from jax import lax
from jax.experimental import pallas as pl
from jax.experimental.pallas import tpu as pltpu
from jax.sharding import PartitionSpec as P

REACH = 4
ITERS = 2
CHIP_REACH = REACH // 2
WINDOW = 2 * CHIP_REACH + 1
F32 = jnp.float32
BF16 = jnp.bfloat16
VMEM = pl.BlockSpec(memory_space=pltpu.VMEM)
HBM = pl.BlockSpec(memory_space=pltpu.HBM)


def hop_offsets(chip):
    near = 1 - 2 * lax.rem(chip, 2)
    far = 2 - 4 * lax.rem(chip // 2, 2)
    return (-near, -far, far, near)


def hop_pairs(ranks):
    chips = ranks // 2
    groups = []
    for step, phase in ((1, 1), (2, 1), (2, 0), (1, 0)):
        pairs = []
        for chip in range(chips - step):
            if (chip // step) % 2 == phase:
                for core in (0, 1):
                    low, high = 2 * chip + core, 2 * (chip + step) + core
                    pairs += [(low, high), (high, low)]
        busy = {source for source, _ in pairs}
        pairs += [(rank, rank ^ 1) for rank in range(ranks) if rank not in busy]
        groups.append(pairs)
    return groups


def bounds(lengths, bores):
    upto = lax.broadcasted_iota(jnp.int32, (bores, bores), 1) <= lax.broadcasted_iota(
        jnp.int32, (bores, bores), 0
    )
    ends = jnp.sum(jnp.where(upto, lengths.astype(F32), 0.0), axis=1, keepdims=True)
    here = lax.broadcasted_iota(jnp.int32, (bores, bores), 1) == lax.broadcasted_iota(
        jnp.int32, (bores, bores), 0
    )
    counts = jnp.sum(jnp.where(here, lengths.astype(F32), 0.0), axis=1, keepdims=True)
    return ends, counts


def compress_kernel(cols_hbm, count_hbm, lengths_hbm, tiles_hbm, *rest):
    outs = rest[: WINDOW]
    cols_ref, count_ref, lengths_ref, slab, tiles, small_sems, sems = rest[WINDOW:]
    small = []
    for index, (source, target) in enumerate(
        ((cols_hbm, cols_ref), (count_hbm, count_ref), (lengths_hbm, lengths_ref))
    ):
        copy = pltpu.make_async_copy(source, target, small_sems.at[index])
        copy.start()
        small.append(copy)
    block_rows, slots, tile = tiles.shape[0], tiles.shape[1], tiles.shape[2]
    bores = slab.shape[1]
    per_chip = 2 * block_rows
    copies = []
    for row in range(block_rows):
        copy = pltpu.make_async_copy(tiles_hbm.at[row], tiles.at[row], sems.at[row])
        copy.start()
        copies.append(copy)
    slab[...] = jnp.zeros_like(slab)
    chip = lax.axis_index("rows") // 2
    for copy in small:
        copy.wait()
    first_block = (chip - CHIP_REACH) * per_chip
    ends, counts = bounds(lengths_ref[...], bores)
    starts = ends - counts
    members = []
    for row in range(block_rows):
        position = (
            lax.broadcasted_iota(jnp.int32, (bores, tile), 1) + row * tile
        ).astype(F32)
        inside = (position >= starts) & (position < ends)
        members.append(inside.astype(F32).astype(BF16))
    empty = jnp.zeros((bores, tile), BF16)
    for row in range(0, block_rows, 2):
        upper = jnp.concatenate([members[row], empty], axis=1)
        under = jnp.concatenate([empty, members[row + 1]], axis=1)
        left = jnp.concatenate([upper, under], axis=0)
        copies[row].wait()
        copies[row + 1].wait()
        for slot in range(0, slots, 2):
            right = jnp.concatenate(
                [
                    jnp.concatenate([tiles[at, slot], tiles[at, slot + 1]], axis=1)
                    for at in (row, row + 1)
                ],
                axis=0,
            )
            product = jnp.dot(left, right, preferred_element_type=F32)
            for i in range(2):
                for j in range(2):
                    place = jnp.where(
                        slot + j < count_ref[row + i],
                        cols_ref[row + i, slot + j] - first_block,
                        WINDOW * per_chip,
                    )
                    slab[place] += product[
                        i * bores : (i + 1) * bores, j * tile : (j + 1) * tile
                    ]
    for out, offset in zip(outs, (0,) + hop_offsets(chip)):
        out[...] = slab[pl.ds((offset + CHIP_REACH) * per_chip, per_chip)]


def split(value):
    high = value.astype(BF16)
    return high, (value - high.astype(F32)).astype(BF16)


def block_of(piece, block, tile):
    if len(piece.shape) == 3:
        return piece[block]
    return piece[:, pl.ds(pl.multiple_of(block * tile, tile), tile)]


def gram_kernel(lengths_ref, recorded_ref, *rest):
    mine, other = rest[:WINDOW], rest[WINDOW : 2 * WINDOW]
    heat_mine, heat_other = rest[2 * WINDOW : 2 * WINDOW + 2]
    outs = rest[2 * WINDOW + 2 : 3 * WINDOW + 2]
    high, low, heat, left, shifted = rest[3 * WINDOW + 2 :]
    blocks, bores, tile = other[0].shape
    me = lax.axis_index("rows")
    chip, core = me // 2, lax.rem(me, 2)
    seg_rows = heat_mine.shape[0]
    offsets = (0,) + hop_offsets(chip)
    for pieces, side in ((mine, core), (other, 1 - core)):
        for piece, offset in zip(pieces, offsets):
            at = pl.multiple_of((offset + CHIP_REACH) * 2 * bores + side * bores, bores)
            for block in range(blocks):
                top, rest_of = split(block_of(piece, block, tile))
                high[pl.ds(at, bores), block * tile : (block + 1) * tile] = top
                low[pl.ds(at, bores), block * tile : (block + 1) * tile] = rest_of
    heat[pl.ds(pl.multiple_of(core * seg_rows, seg_rows), seg_rows)] = heat_mine[...]
    heat[pl.ds(pl.multiple_of((1 - core) * seg_rows, seg_rows), seg_rows)] = heat_other[...]
    for slot in range(WINDOW):
        at = pl.multiple_of(slot * 2 * bores + core * bores, bores)
        left[slot * bores : (slot + 1) * bores] = high[pl.ds(at, bores)]
        left[(WINDOW + slot) * bores : (WINDOW + slot + 1) * bores] = low[pl.ds(at, bores)]
    rows = WINDOW * bores
    transposed = (((1,), (1,)), ((), ()))
    both = lax.dot_general(left[...], high[...], transposed, preferred_element_type=F32)
    cross = lax.dot_general(left[:rows], low[...], transposed, preferred_element_type=F32)
    gram = both[:rows] + both[rows:] + cross
    warm = jnp.dot(left[...], heat[...], preferred_element_type=F32)
    warm = warm[:rows] + warm[rows:]
    span = 2 * bores
    width = 3 * 2 * span
    lane = lax.broadcasted_iota(jnp.int32, (bores, width), 1)
    padded = jnp.concatenate(
        [gram, jnp.zeros((rows, width - WINDOW * span), F32)], axis=1
    )
    for slot in range(WINDOW):
        offset = slot - CHIP_REACH
        base = padded[slot * bores : (slot + 1) * bores]
        odd = lax.rem(chip + offset + 2, 2)
        places = []
        for parity in (0, 1):
            shift = (CHIP_REACH - offset + parity) * span
            moved = pltpu.roll(base, shift % width, 1) if shift % width else base
            keep = (lane >= shift) & (lane < (WINDOW + parity) * span)
            places.append(jnp.where(keep, moved, 0.0))
        shifted[slot, :, :width] = jnp.where(odd == 1, places[1], places[0])
        shifted[slot, :, width:] = warm[slot * bores : (slot + 1) * bores]
    _, counts = bounds(lengths_ref[...], bores)
    odd = lax.rem(chip, 2)
    free = ((odd == 1) & (lane < span)) | ((odd == 0) & (lane >= WINDOW * span))
    shifted[CHIP_REACH, :, :width] = jnp.where(
        free, counts, shifted[CHIP_REACH, :, :width]
    )
    shifted[CHIP_REACH, :, width:] = (
        shifted[CHIP_REACH, :, width:] - counts * recorded_ref[...]
    )
    for out, offset in zip(outs, offsets):
        out[...] = shifted[offset + CHIP_REACH]


def transpose_kernel(*rest):
    mine, other = rest[:WINDOW], rest[WINDOW : 2 * WINDOW]
    high, low = rest[2 * WINDOW : 2 * WINDOW + 2]
    (rows_of,) = rest[2 * WINDOW + 2 :]
    blocks, bores, tile = other[0].shape
    own_blocks = blocks // 2
    me = lax.axis_index("rows")
    chip, core = me // 2, lax.rem(me, 2)
    for pieces, side in ((mine, core), (other, 1 - core)):
        for piece, offset in zip(pieces, (0,) + hop_offsets(chip)):
            at = pl.multiple_of((offset + CHIP_REACH) * 2 * bores + side * bores, bores)
            for block in range(own_blocks):
                rows_of[block, pl.ds(at, bores)] = block_of(
                    piece, core * own_blocks + block, tile
                )
    for block in range(own_blocks):
        top, rest_of = split(rows_of[block].T)
        high[block * tile : (block + 1) * tile] = top
        low[block * tile : (block + 1) * tile] = rest_of


def descend_kernel(ranks, places, heat_hbm, high_ref, low_ref, *rest):
    pieces, rest = rest[: len(places)], rest[len(places) :]
    heat_out, misfit_out = rest[:2]
    lower, band, counts, misfit, warm, shares, heat_ref, heat_sem = rest[2:]
    fetch = pltpu.make_async_copy(heat_hbm, heat_ref, heat_sem)
    fetch.start()
    bores, columns = misfit_out.shape
    width = lower.shape[1]
    plane = 4 * bores
    planes = ranks // 4
    span = 2 * bores
    me = lax.axis_index("rows")
    lane = lax.broadcasted_iota(jnp.int32, (bores, width), 1)
    for indices, piece in zip(places, pieces):
        for part, index in enumerate(indices):
            here = slice(part * bores, (part + 1) * bores)
            rank = jnp.bitwise_xor(me, index)
            at = pl.multiple_of(rank * bores, bores)
            odd = lax.rem(rank // 2, 2) == 1
            count = jnp.where(odd, piece[here, :1], piece[here, width - 1 : width])
            free = (odd & (lane < span)) | (
                jnp.logical_not(odd) & (lane >= WINDOW * span)
            )
            lower[pl.ds(at, bores)] = jnp.where(free, 0.0, piece[here, :width])
            misfit[pl.ds(at, bores)] = piece[here, width:] / count
            counts[pl.ds(at, bores)] = jnp.broadcast_to(count, (bores, columns))
    half_row = lax.broadcasted_iota(jnp.int32, (plane, plane), 0) < span
    half_col = lax.broadcasted_iota(jnp.int32, (plane, plane), 1) >= span
    for p in range(planes):
        rows = lower[p * plane : (p + 1) * plane]
        diagonal = rows[:, 2 * plane :]
        diagonal = jnp.where(half_row & half_col, diagonal.T, diagonal)
        after = []
        for step in (1, 2):
            if p + step < planes:
                following = lower[(p + step) * plane : (p + step + 1) * plane]
                after.append(following[:, (2 - step) * plane : (3 - step) * plane].T)
            else:
                after.append(jnp.zeros((plane, plane), F32))
        whole = [rows[:, :plane], rows[:, plane : 2 * plane], diagonal] + after
        for index, part in enumerate(whole):
            top, rest_of = split(part)
            band[p, :plane, index * plane : (index + 1) * plane] = top
            band[p, plane:, index * plane : (index + 1) * plane] = rest_of
    shares[:, : 2 * plane] = jnp.zeros((ITERS, 2 * plane, columns), BF16)
    shares[:, (planes + 2) * plane :] = jnp.zeros((ITERS, 2 * plane, columns), BF16)
    steps = []
    for iteration in range(ITERS):
        shares[iteration, 2 * plane : (planes + 2) * plane] = (
            misfit[...] / counts[...]
        ).astype(BF16)
        power = jnp.zeros((plane, columns), F32)
        curvature = jnp.zeros((plane, columns), F32)
        for p in range(planes):
            both = jnp.dot(
                band[p],
                shares[iteration, p * plane : (p + 5) * plane],
                preferred_element_type=F32,
            )
            swept = both[:plane] + both[plane:]
            here = shares[iteration, (p + 2) * plane : (p + 3) * plane].astype(F32)
            image = swept / counts[p * plane : (p + 1) * plane]
            warm[p * plane : (p + 1) * plane] = image
            power = power + here * swept
            curvature = curvature + image * image
        step = jnp.sum(power) / (jnp.sum(curvature) + 1e-06)
        steps.append(step)
        misfit[...] = misfit[...] - step * warm[...]
    misfit_out[...] = misfit[pl.ds(pl.multiple_of(me * bores, bores), bores)]
    first = pl.multiple_of((me // 2 - CHIP_REACH) * span + 2 * plane, span)
    fetch.wait()
    heat = heat_ref[...]
    for iteration in range(ITERS):
        near = shares[iteration, pl.ds(first, WINDOW * span)]
        gradient = jnp.dot(high_ref[...], near, preferred_element_type=F32) + jnp.dot(
            low_ref[...], near, preferred_element_type=F32
        )
        heat = heat - steps[iteration] * gradient
    heat_out[...] = heat


def on_device(
    ranks, response_tiles, tile_cols, tile_count, heat_start, recorded, bore_lengths
):
    block_rows, slots, tile = response_tiles.shape[:3]
    seg_rows, columns = heat_start.shape
    bores = bore_lengths.shape[1]
    per_chip = 2 * block_rows
    rows = WINDOW * bores
    span = 2 * bores
    width = 6 * span
    hops = hop_pairs(ranks)
    limit = pltpu.CompilerParams(vmem_limit_bytes=48 << 20)

    def send(value, pairs):
        return lax.ppermute(value, "rows", pairs)

    def swap(value, bit):
        return send(value, [(rank, rank ^ bit) for rank in range(ranks)])

    piece = jax.ShapeDtypeStruct((per_chip, bores, tile), F32)
    sent = pl.pallas_call(
        compress_kernel,
        out_shape=(piece,) * WINDOW,
        in_specs=[HBM] * 4,
        out_specs=(VMEM,) * WINDOW,
        scratch_shapes=[
            pltpu.SMEM(tile_cols.shape, jnp.int32),
            pltpu.SMEM(tile_count.shape, jnp.int32),
            pltpu.VMEM(bore_lengths.shape, jnp.int32),
            pltpu.VMEM((WINDOW * per_chip + 1, bores, tile), F32),
            pltpu.VMEM((block_rows, slots, tile, tile), BF16),
            pltpu.SemaphoreType.DMA((3,)),
            pltpu.SemaphoreType.DMA((block_rows,)),
        ],
        compiler_params=pltpu.CompilerParams(vmem_limit_bytes=60 << 20),
        name="compress",
    )(tile_cols, tile_count, bore_lengths, response_tiles)
    mine = [sent[0]] + [send(value, pairs) for value, pairs in zip(sent[1:], hops)]
    mine[1], heat_late, own = lax.optimization_barrier((mine[1], heat_start, mine[0]))
    heat_low = heat_late.astype(BF16)
    heat_other = swap(heat_low, 1)
    own = own.transpose(1, 0, 2).reshape(bores, per_chip * tile)
    mine[2], own = lax.optimization_barrier((mine[2], own))
    other = [swap(value, 1) for value in mine]
    mine[0] = own
    packed = jax.ShapeDtypeStruct((bores, width + columns), F32)
    partial = pl.pallas_call(
        gram_kernel,
        out_shape=(packed,) * WINDOW,
        in_specs=[VMEM] * (2 * WINDOW + 4),
        out_specs=(VMEM,) * WINDOW,
        scratch_shapes=[
            pltpu.VMEM((WINDOW * span, per_chip * tile), BF16),
            pltpu.VMEM((WINDOW * span, per_chip * tile), BF16),
            pltpu.VMEM((2 * seg_rows, columns), BF16),
            pltpu.VMEM((2 * rows, per_chip * tile), BF16),
            pltpu.VMEM((WINDOW, bores, width + columns), F32),
        ],
        compiler_params=limit,
        name="gram",
    )(bore_lengths, recorded, *mine, *other, heat_low, heat_other)
    parts = [partial[0]] + [send(value, pairs) for value, pairs in zip(partial[1:], hops)]
    turned = jax.ShapeDtypeStruct((seg_rows, WINDOW * span), BF16)
    high, low = pl.pallas_call(
        transpose_kernel,
        out_shape=(turned, turned),
        in_specs=[VMEM] * (2 * WINDOW),
        out_specs=(VMEM, VMEM),
        scratch_shapes=[pltpu.VMEM((block_rows, WINDOW * span, tile), F32)],
        compiler_params=limit,
        name="turn",
    )(*mine, *other)
    total, high, low = lax.optimization_barrier((parts[0], high, low))
    for part in parts[1:]:
        total = total + part
    column = {0: total}
    for index in (8, 4, 12):
        if index < ranks:
            column[index] = swap(total, index)
    bit = 16
    while bit < ranks:
        column.update({index ^ bit: swap(value, bit) for index, value in list(column.items())})
        bit *= 2
    beside = {index: swap(value, 2) for index, value in column.items()}
    across = {
        index: swap(jnp.concatenate([value, beside[index]], axis=0), 1)
        for index, value in column.items()
    }
    places = tuple(
        [(index,) for index in column]
        + [(index ^ 2,) for index in column]
        + [(index ^ 1, index ^ 3) for index in column]
    )
    gathered = list(column.values()) + list(beside.values()) + list(across.values())
    return pl.pallas_call(
        functools.partial(descend_kernel, ranks, places),
        out_shape=(
            jax.ShapeDtypeStruct((seg_rows, columns), F32),
            jax.ShapeDtypeStruct((bores, columns), F32),
        ),
        in_specs=[HBM] + [VMEM] * (2 + len(gathered)),
        out_specs=(VMEM, VMEM),
        scratch_shapes=[
            pltpu.VMEM((ranks * bores, width), F32),
            pltpu.VMEM((ranks // 4, 8 * bores, 20 * bores), BF16),
            pltpu.VMEM((ranks * bores, columns), F32),
            pltpu.VMEM((ranks * bores, columns), F32),
            pltpu.VMEM((ranks * bores, columns), F32),
            pltpu.VMEM((ITERS, (ranks + 16) * bores, columns), BF16),
            pltpu.VMEM((seg_rows, columns), F32),
            pltpu.SemaphoreType.DMA,
        ],
        compiler_params=limit,
        name="descend",
    )(heat_start, high, low, *gathered)


def solution(mesh):
    placed = (
        P(("groups", "rows"), None, None, None),
        P(("groups", "rows"), None),
        P(("groups", "rows")),
        P(("groups", "rows"), None),
        P(("groups", "rows"), None),
        P(("groups", "rows"), None),
    )
    return jax.shard_map(
        functools.partial(on_device, mesh.shape["rows"]),
        mesh=mesh,
        in_specs=placed,
        out_specs=(P(("groups", "rows"), None), P(("groups", "rows"), None)),
        check_vma=False,
    )
```

```python
import functools

import jax
import jax.numpy as jnp
from jax import lax
from jax.experimental import pallas as pl
from jax.experimental.pallas import tpu as pltpu
from jax.sharding import PartitionSpec as P

REACH = 4
ITERS = 2
CHIP_REACH = REACH // 2
WINDOW = 2 * CHIP_REACH + 1
F32 = jnp.float32
BF16 = jnp.bfloat16
VMEM = pl.BlockSpec(memory_space=pltpu.VMEM)
HBM = pl.BlockSpec(memory_space=pltpu.HBM)


def hop_offsets(chip):
    near = 1 - 2 * lax.rem(chip, 2)
    far = 2 - 4 * lax.rem(chip // 2, 2)
    return (-near, -far, far, near)


def hop_pairs(ranks):
    chips = ranks // 2
    groups = []
    for step, phase in ((1, 1), (2, 1), (2, 0), (1, 0)):
        pairs = []
        for chip in range(chips - step):
            if (chip // step) % 2 == phase:
                for core in (0, 1):
                    low, high = 2 * chip + core, 2 * (chip + step) + core
                    pairs += [(low, high), (high, low)]
        busy = {source for source, _ in pairs}
        pairs += [(rank, rank ^ 1) for rank in range(ranks) if rank not in busy]
        groups.append(pairs)
    return groups


def bounds(lengths, bores):
    upto = lax.broadcasted_iota(jnp.int32, (bores, bores), 1) <= lax.broadcasted_iota(
        jnp.int32, (bores, bores), 0
    )
    ends = jnp.sum(jnp.where(upto, lengths.astype(F32), 0.0), axis=1, keepdims=True)
    here = lax.broadcasted_iota(jnp.int32, (bores, bores), 1) == lax.broadcasted_iota(
        jnp.int32, (bores, bores), 0
    )
    counts = jnp.sum(jnp.where(here, lengths.astype(F32), 0.0), axis=1, keepdims=True)
    return ends, counts


def compress_kernel(cols_hbm, count_hbm, lengths_hbm, tiles_hbm, *rest):
    outs = rest[: WINDOW]
    cols_ref, count_ref, lengths_ref, slab, tiles, small_sems, sems = rest[WINDOW:]
    small = []
    for index, (source, target) in enumerate(
        ((cols_hbm, cols_ref), (count_hbm, count_ref), (lengths_hbm, lengths_ref))
    ):
        copy = pltpu.make_async_copy(source, target, small_sems.at[index])
        copy.start()
        small.append(copy)
    block_rows, slots, tile = tiles.shape[0], tiles.shape[1], tiles.shape[2]
    bores = slab.shape[1]
    per_chip = 2 * block_rows
    copies = []
    for row in range(block_rows):
        copy = pltpu.make_async_copy(tiles_hbm.at[row], tiles.at[row], sems.at[row])
        copy.start()
        copies.append(copy)
    slab[...] = jnp.zeros_like(slab)
    chip = lax.axis_index("rows") // 2
    for copy in small:
        copy.wait()
    first_block = (chip - CHIP_REACH) * per_chip
    ends, counts = bounds(lengths_ref[...], bores)
    starts = ends - counts
    members = []
    for row in range(block_rows):
        position = (
            lax.broadcasted_iota(jnp.int32, (bores, tile), 1) + row * tile
        ).astype(F32)
        inside = (position >= starts) & (position < ends)
        members.append(inside.astype(F32).astype(BF16))
    empty = jnp.zeros((bores, tile), BF16)
    for row in range(0, block_rows, 2):
        upper = jnp.concatenate([members[row], empty], axis=1)
        under = jnp.concatenate([empty, members[row + 1]], axis=1)
        left = jnp.concatenate([upper, under], axis=0)
        copies[row].wait()
        copies[row + 1].wait()
        for slot in range(0, slots, 2):
            right = jnp.concatenate(
                [
                    jnp.concatenate([tiles[at, slot], tiles[at, slot + 1]], axis=1)
                    for at in (row, row + 1)
                ],
                axis=0,
            )
            product = jnp.dot(left, right, preferred_element_type=F32)
            for i in range(2):
                for j in range(2):
                    place = jnp.where(
                        slot + j < count_ref[row + i],
                        cols_ref[row + i, slot + j] - first_block,
                        WINDOW * per_chip,
                    )
                    slab[place] += product[
                        i * bores : (i + 1) * bores, j * tile : (j + 1) * tile
                    ]
    for out, offset in zip(outs, (0,) + hop_offsets(chip)):
        out[...] = slab[pl.ds((offset + CHIP_REACH) * per_chip, per_chip)]


def split(value):
    high = value.astype(BF16)
    return high, (value - high.astype(F32)).astype(BF16)


def block_of(piece, block, tile):
    if len(piece.shape) == 3:
        return piece[block]
    return piece[:, pl.ds(pl.multiple_of(block * tile, tile), tile)]


def gram_kernel(lengths_ref, recorded_ref, *rest):
    mine, other = rest[:WINDOW], rest[WINDOW : 2 * WINDOW]
    heat_mine, heat_other = rest[2 * WINDOW : 2 * WINDOW + 2]
    outs = rest[2 * WINDOW + 2 : 3 * WINDOW + 2]
    high, low, heat, left, shifted = rest[3 * WINDOW + 2 :]
    blocks, bores, tile = other[0].shape
    me = lax.axis_index("rows")
    chip, core = me // 2, lax.rem(me, 2)
    seg_rows = heat_mine.shape[0]
    offsets = (0,) + hop_offsets(chip)
    for pieces, side in ((mine, core), (other, 1 - core)):
        for piece, offset in zip(pieces, offsets):
            at = pl.multiple_of((offset + CHIP_REACH) * 2 * bores + side * bores, bores)
            for block in range(blocks):
                top, rest_of = split(block_of(piece, block, tile))
                high[pl.ds(at, bores), block * tile : (block + 1) * tile] = top
                low[pl.ds(at, bores), block * tile : (block + 1) * tile] = rest_of
    heat[pl.ds(pl.multiple_of(core * seg_rows, seg_rows), seg_rows)] = heat_mine[...]
    heat[pl.ds(pl.multiple_of((1 - core) * seg_rows, seg_rows), seg_rows)] = heat_other[...]
    for slot in range(WINDOW):
        at = pl.multiple_of(slot * 2 * bores + core * bores, bores)
        left[slot * bores : (slot + 1) * bores] = high[pl.ds(at, bores)]
        left[(WINDOW + slot) * bores : (WINDOW + slot + 1) * bores] = low[pl.ds(at, bores)]
    rows = WINDOW * bores
    transposed = (((1,), (1,)), ((), ()))
    both = lax.dot_general(left[...], high[...], transposed, preferred_element_type=F32)
    cross = lax.dot_general(left[:rows], low[...], transposed, preferred_element_type=F32)
    gram = both[:rows] + both[rows:] + cross
    warm = jnp.dot(left[...], heat[...], preferred_element_type=F32)
    warm = warm[:rows] + warm[rows:]
    span = 2 * bores
    width = 3 * 2 * span
    lane = lax.broadcasted_iota(jnp.int32, (bores, width), 1)
    padded = jnp.concatenate(
        [gram, jnp.zeros((rows, width - WINDOW * span), F32)], axis=1
    )
    for slot in range(WINDOW):
        offset = slot - CHIP_REACH
        base = padded[slot * bores : (slot + 1) * bores]
        odd = lax.rem(chip + offset + 2, 2)
        places = []
        for parity in (0, 1):
            shift = (CHIP_REACH - offset + parity) * span
            moved = pltpu.roll(base, shift % width, 1) if shift % width else base
            keep = (lane >= shift) & (lane < (WINDOW + parity) * span)
            places.append(jnp.where(keep, moved, 0.0))
        shifted[slot, :, :width] = jnp.where(odd == 1, places[1], places[0])
        shifted[slot, :, width:] = warm[slot * bores : (slot + 1) * bores]
    _, counts = bounds(lengths_ref[...], bores)
    odd = lax.rem(chip, 2)
    free = ((odd == 1) & (lane < span)) | ((odd == 0) & (lane >= WINDOW * span))
    shifted[CHIP_REACH, :, :width] = jnp.where(
        free, counts, shifted[CHIP_REACH, :, :width]
    )
    shifted[CHIP_REACH, :, width:] = (
        shifted[CHIP_REACH, :, width:] - counts * recorded_ref[...]
    )
    for out, offset in zip(outs, offsets):
        out[...] = shifted[offset + CHIP_REACH]


def transpose_kernel(*rest):
    mine, other = rest[:WINDOW], rest[WINDOW : 2 * WINDOW]
    high, low = rest[2 * WINDOW : 2 * WINDOW + 2]
    (rows_of,) = rest[2 * WINDOW + 2 :]
    blocks, bores, tile = other[0].shape
    own_blocks = blocks // 2
    me = lax.axis_index("rows")
    chip, core = me // 2, lax.rem(me, 2)
    for pieces, side in ((mine, core), (other, 1 - core)):
        for piece, offset in zip(pieces, (0,) + hop_offsets(chip)):
            at = pl.multiple_of((offset + CHIP_REACH) * 2 * bores + side * bores, bores)
            for block in range(own_blocks):
                rows_of[block, pl.ds(at, bores)] = block_of(
                    piece, core * own_blocks + block, tile
                )
    for block in range(own_blocks):
        top, rest_of = split(rows_of[block].T)
        high[block * tile : (block + 1) * tile] = top
        low[block * tile : (block + 1) * tile] = rest_of


def descend_kernel(ranks, places, heat_hbm, high_ref, low_ref, *rest):
    pieces, rest = rest[: len(places)], rest[len(places) :]
    heat_out, misfit_out = rest[:2]
    lower, band, counts, misfit, warm, shares, heat_ref, heat_sem = rest[2:]
    fetch = pltpu.make_async_copy(heat_hbm, heat_ref, heat_sem)
    fetch.start()
    bores, columns = misfit_out.shape
    width = lower.shape[1]
    plane = 4 * bores
    planes = ranks // 4
    span = 2 * bores
    me = lax.axis_index("rows")
    lane = lax.broadcasted_iota(jnp.int32, (bores, width), 1)
    for indices, piece in zip(places, pieces):
        for part, index in enumerate(indices):
            here = slice(part * bores, (part + 1) * bores)
            rank = jnp.bitwise_xor(me, index)
            at = pl.multiple_of(rank * bores, bores)
            odd = lax.rem(rank // 2, 2) == 1
            count = jnp.where(odd, piece[here, :1], piece[here, width - 1 : width])
            free = (odd & (lane < span)) | (
                jnp.logical_not(odd) & (lane >= WINDOW * span)
            )
            lower[pl.ds(at, bores)] = jnp.where(free, 0.0, piece[here, :width])
            misfit[pl.ds(at, bores)] = piece[here, width:] / count
            counts[pl.ds(at, bores)] = jnp.broadcast_to(count, (bores, columns))
    half_row = lax.broadcasted_iota(jnp.int32, (plane, plane), 0) < span
    half_col = lax.broadcasted_iota(jnp.int32, (plane, plane), 1) >= span
    for p in range(planes):
        rows = lower[p * plane : (p + 1) * plane]
        diagonal = rows[:, 2 * plane :]
        diagonal = jnp.where(half_row & half_col, diagonal.T, diagonal)
        whole = {0: diagonal}
        for step in (1, 2):
            if p - step >= 0:
                whole[-step] = rows[:, (2 - step) * plane : (3 - step) * plane]
            if p + step < planes:
                following = lower[(p + step) * plane : (p + step + 1) * plane]
                whole[step] = following[:, (2 - step) * plane : (3 - step) * plane].T
        for step, part in whole.items():
            top, rest_of = split(part)
            at = (step + 2) * plane
            band[p, :plane, at : at + plane] = top
            band[p, plane:, at : at + plane] = rest_of
    shares[: 2 * plane] = jnp.zeros((2 * plane, ITERS * columns), BF16)
    shares[(planes + 2) * plane :] = jnp.zeros((2 * plane, ITERS * columns), BF16)
    first = pl.multiple_of((me // 2 - CHIP_REACH) * span + 2 * plane, span)
    steps = []
    for iteration in range(ITERS):
        lanes = slice(iteration * columns, (iteration + 1) * columns)
        shares[2 * plane : (planes + 2) * plane, lanes] = (
            misfit[...] / counts[...]
        ).astype(BF16)
        if iteration == ITERS - 1:
            near = shares[pl.ds(first, WINDOW * span)]
            gradients = jnp.dot(
                high_ref[...], near, preferred_element_type=F32
            ) + jnp.dot(low_ref[...], near, preferred_element_type=F32)
        power = jnp.zeros((plane, columns), F32)
        curvature = jnp.zeros((plane, columns), F32)
        for p in range(planes):
            start, stop = max(p - 2, 0), min(p + 3, planes)
            both = jnp.dot(
                band[p, :, (start - p + 2) * plane : (stop - p + 2) * plane],
                shares[(start + 2) * plane : (stop + 2) * plane, lanes],
                preferred_element_type=F32,
            )
            swept = both[:plane] + both[plane:]
            here = shares[(p + 2) * plane : (p + 3) * plane, lanes].astype(F32)
            image = swept / counts[p * plane : (p + 1) * plane]
            warm[p * plane : (p + 1) * plane] = image
            power = power + here * swept
            curvature = curvature + image * image
        step = jnp.sum(power) / (jnp.sum(curvature) + 1e-06)
        steps.append(step)
        if iteration < ITERS - 1:
            misfit[...] = misfit[...] - step * warm[...]
    mine = pl.ds(pl.multiple_of(me * bores, bores), bores)
    misfit_out[...] = misfit[mine] - steps[-1] * warm[mine]
    fetch.wait()
    heat = heat_ref[...]
    for iteration in range(ITERS):
        heat = heat - steps[iteration] * gradients[
            :, iteration * columns : (iteration + 1) * columns
        ]
    heat_out[...] = heat


def on_device(
    ranks, response_tiles, tile_cols, tile_count, heat_start, recorded, bore_lengths
):
    block_rows, slots, tile = response_tiles.shape[:3]
    seg_rows, columns = heat_start.shape
    bores = bore_lengths.shape[1]
    per_chip = 2 * block_rows
    rows = WINDOW * bores
    span = 2 * bores
    width = 6 * span
    hops = hop_pairs(ranks)
    limit = pltpu.CompilerParams(vmem_limit_bytes=48 << 20)

    def send(value, pairs):
        return lax.ppermute(value, "rows", pairs)

    def swap(value, bit):
        return send(value, [(rank, rank ^ bit) for rank in range(ranks)])

    piece = jax.ShapeDtypeStruct((per_chip, bores, tile), F32)
    sent = pl.pallas_call(
        compress_kernel,
        out_shape=(piece,) * WINDOW,
        in_specs=[HBM] * 4,
        out_specs=(VMEM,) * WINDOW,
        scratch_shapes=[
            pltpu.SMEM(tile_cols.shape, jnp.int32),
            pltpu.SMEM(tile_count.shape, jnp.int32),
            pltpu.VMEM(bore_lengths.shape, jnp.int32),
            pltpu.VMEM((WINDOW * per_chip + 1, bores, tile), F32),
            pltpu.VMEM((block_rows, slots, tile, tile), BF16),
            pltpu.SemaphoreType.DMA((3,)),
            pltpu.SemaphoreType.DMA((block_rows,)),
        ],
        compiler_params=pltpu.CompilerParams(vmem_limit_bytes=60 << 20),
        name="compress",
    )(tile_cols, tile_count, bore_lengths, response_tiles)
    mine = [sent[0]] + [send(value, pairs) for value, pairs in zip(sent[1:], hops)]
    mine[1], heat_late, own = lax.optimization_barrier((mine[1], heat_start, mine[0]))
    heat_low = heat_late.astype(BF16)
    heat_other = swap(heat_low, 1)
    own = own.transpose(1, 0, 2).reshape(bores, per_chip * tile)
    mine[2], own = lax.optimization_barrier((mine[2], own))
    other = [swap(value, 1) for value in mine]
    mine[0] = own
    packed = jax.ShapeDtypeStruct((bores, width + columns), F32)
    partial = pl.pallas_call(
        gram_kernel,
        out_shape=(packed,) * WINDOW,
        in_specs=[VMEM] * (2 * WINDOW + 4),
        out_specs=(VMEM,) * WINDOW,
        scratch_shapes=[
            pltpu.VMEM((WINDOW * span, per_chip * tile), BF16),
            pltpu.VMEM((WINDOW * span, per_chip * tile), BF16),
            pltpu.VMEM((2 * seg_rows, columns), BF16),
            pltpu.VMEM((2 * rows, per_chip * tile), BF16),
            pltpu.VMEM((WINDOW, bores, width + columns), F32),
        ],
        compiler_params=limit,
        name="gram",
    )(bore_lengths, recorded, *mine, *other, heat_low, heat_other)
    parts = [partial[0]] + [send(value, pairs) for value, pairs in zip(partial[1:], hops)]
    turned = jax.ShapeDtypeStruct((seg_rows, WINDOW * span), BF16)
    high, low = pl.pallas_call(
        transpose_kernel,
        out_shape=(turned, turned),
        in_specs=[VMEM] * (2 * WINDOW),
        out_specs=(VMEM, VMEM),
        scratch_shapes=[pltpu.VMEM((block_rows, WINDOW * span, tile), F32)],
        compiler_params=limit,
        name="turn",
    )(*mine, *other)
    total, high, low = lax.optimization_barrier((parts[0], high, low))
    for part in parts[1:]:
        total = total + part
    column = {0: total}
    for index in (8, 4, 12):
        if index < ranks:
            column[index] = swap(total, index)
    bit = 16
    while bit < ranks:
        column.update({index ^ bit: swap(value, bit) for index, value in list(column.items())})
        bit *= 2
    beside = {index: swap(value, 2) for index, value in column.items()}
    across = {
        index: swap(jnp.concatenate([value, beside[index]], axis=0), 1)
        for index, value in column.items()
    }
    places = tuple(
        [(index,) for index in column]
        + [(index ^ 2,) for index in column]
        + [(index ^ 1, index ^ 3) for index in column]
    )
    gathered = list(column.values()) + list(beside.values()) + list(across.values())
    return pl.pallas_call(
        functools.partial(descend_kernel, ranks, places),
        out_shape=(
            jax.ShapeDtypeStruct((seg_rows, columns), F32),
            jax.ShapeDtypeStruct((bores, columns), F32),
        ),
        in_specs=[HBM] + [VMEM] * (2 + len(gathered)),
        out_specs=(VMEM, VMEM),
        scratch_shapes=[
            pltpu.VMEM((ranks * bores, width), F32),
            pltpu.VMEM((ranks // 4, 8 * bores, 20 * bores), BF16),
            pltpu.VMEM((ranks * bores, columns), F32),
            pltpu.VMEM((ranks * bores, columns), F32),
            pltpu.VMEM((ranks * bores, columns), F32),
            pltpu.VMEM(((ranks + 16) * bores, ITERS * columns), BF16),
            pltpu.VMEM((seg_rows, columns), F32),
            pltpu.SemaphoreType.DMA,
        ],
        compiler_params=limit,
        name="descend",
    )(heat_start, high, low, *gathered)


def solution(mesh):
    placed = (
        P(("groups", "rows"), None, None, None),
        P(("groups", "rows"), None),
        P(("groups", "rows")),
        P(("groups", "rows"), None),
        P(("groups", "rows"), None),
        P(("groups", "rows"), None),
    )
    return jax.shard_map(
        functools.partial(on_device, mesh.shape["rows"]),
        mesh=mesh,
        in_specs=placed,
        out_specs=(P(("groups", "rows"), None), P(("groups", "rows"), None)),
        check_vma=False,
    )
```

```python
import functools

import jax
import jax.numpy as jnp
from jax import lax
from jax.experimental import pallas as pl
from jax.experimental.pallas import tpu as pltpu
from jax.sharding import PartitionSpec as P

REACH = 4
ITERS = 2
CHIP_REACH = REACH // 2
WINDOW = 2 * CHIP_REACH + 1
F32 = jnp.float32
BF16 = jnp.bfloat16
I16 = jnp.int16
CODE_BITS = 14.0
VMEM = pl.BlockSpec(memory_space=pltpu.VMEM)
HBM = pl.BlockSpec(memory_space=pltpu.HBM)


def hop_offsets(chip):
    near = 1 - 2 * lax.rem(chip, 2)
    far = 2 - 4 * lax.rem(chip // 2, 2)
    return (-near, -far, far, near)


def hop_pairs(ranks):
    chips = ranks // 2
    groups = []
    for step, phase in ((1, 1), (2, 1), (2, 0), (1, 0)):
        pairs = []
        for chip in range(chips - step):
            if (chip // step) % 2 == phase:
                for core in (0, 1):
                    low, high = 2 * chip + core, 2 * (chip + step) + core
                    pairs += [(low, high), (high, low)]
        busy = {source for source, _ in pairs}
        pairs += [(rank, rank ^ 1) for rank in range(ranks) if rank not in busy]
        groups.append(pairs)
    return groups


def bounds(lengths, bores):
    upto = lax.broadcasted_iota(jnp.int32, (bores, bores), 1) <= lax.broadcasted_iota(
        jnp.int32, (bores, bores), 0
    )
    ends = jnp.sum(jnp.where(upto, lengths.astype(F32), 0.0), axis=1, keepdims=True)
    here = lax.broadcasted_iota(jnp.int32, (bores, bores), 1) == lax.broadcasted_iota(
        jnp.int32, (bores, bores), 0
    )
    counts = jnp.sum(jnp.where(here, lengths.astype(F32), 0.0), axis=1, keepdims=True)
    return ends, counts


def compress_kernel(cols_hbm, count_hbm, lengths_hbm, tiles_hbm, *rest):
    outs = rest[: WINDOW]
    cols_ref, count_ref, lengths_ref, slab, tiles, small_sems, sems = rest[WINDOW:]
    small = []
    for index, (source, target) in enumerate(
        ((cols_hbm, cols_ref), (count_hbm, count_ref), (lengths_hbm, lengths_ref))
    ):
        copy = pltpu.make_async_copy(source, target, small_sems.at[index])
        copy.start()
        small.append(copy)
    block_rows, slots, tile = tiles.shape[0], tiles.shape[1], tiles.shape[2]
    bores = slab.shape[1]
    per_chip = 2 * block_rows
    copies = []
    for row in range(block_rows):
        copy = pltpu.make_async_copy(tiles_hbm.at[row], tiles.at[row], sems.at[row])
        copy.start()
        copies.append(copy)
    slab[...] = jnp.zeros_like(slab)
    chip = lax.axis_index("rows") // 2
    for copy in small:
        copy.wait()
    first_block = (chip - CHIP_REACH) * per_chip
    ends, counts = bounds(lengths_ref[...], bores)
    starts = ends - counts
    members = []
    for row in range(block_rows):
        position = (
            lax.broadcasted_iota(jnp.int32, (bores, tile), 1) + row * tile
        ).astype(F32)
        inside = (position >= starts) & (position < ends)
        members.append(inside.astype(F32).astype(BF16))
    empty = jnp.zeros((bores, tile), BF16)
    for row in range(0, block_rows, 2):
        upper = jnp.concatenate([members[row], empty], axis=1)
        under = jnp.concatenate([empty, members[row + 1]], axis=1)
        left = jnp.concatenate([upper, under], axis=0)
        copies[row].wait()
        copies[row + 1].wait()
        for slot in range(0, slots, 2):
            right = jnp.concatenate(
                [
                    jnp.concatenate([tiles[at, slot], tiles[at, slot + 1]], axis=1)
                    for at in (row, row + 1)
                ],
                axis=0,
            )
            product = jnp.dot(left, right, preferred_element_type=F32)
            for i in range(2):
                for j in range(2):
                    place = jnp.where(
                        slot + j < count_ref[row + i],
                        cols_ref[row + i, slot + j] - first_block,
                        WINDOW * per_chip,
                    )
                    slab[place] += product[
                        i * bores : (i + 1) * bores, j * tile : (j + 1) * tile
                    ]
    largest = jnp.max(jnp.abs(slab[: WINDOW * per_chip]), axis=0)
    largest = jnp.max(largest, axis=1, keepdims=True)
    exponent = jnp.ceil(jnp.log2(jnp.maximum(largest, 1e-30)))
    scale = jnp.broadcast_to(jnp.exp2(CODE_BITS - exponent), (bores, tile))
    exponent = jnp.broadcast_to(exponent, (bores, tile)).astype(jnp.int32).astype(I16)
    for out, offset in zip(outs, (0,) + hop_offsets(chip)):
        for block in range(per_chip):
            value = slab[(offset + CHIP_REACH) * per_chip + block]
            out[block] = jnp.round(value * scale).astype(jnp.int32).astype(I16)
        out[per_chip] = exponent


def split(value):
    high = value.astype(BF16)
    return high, (value - high.astype(F32)).astype(BF16)


def block_of(piece, block, tile):
    if len(piece.shape) == 3:
        code = piece[block]
    else:
        code = piece[:, pl.ds(pl.multiple_of(block * tile, tile), tile)]
    return code.astype(jnp.int32).astype(F32)


def gram_kernel(lengths_ref, recorded_ref, *rest):
    mine, other = rest[:WINDOW], rest[WINDOW : 2 * WINDOW]
    heat_mine, heat_other = rest[2 * WINDOW : 2 * WINDOW + 2]
    outs = rest[2 * WINDOW + 2 : 3 * WINDOW + 2]
    high, low, heat, left, shifted = rest[3 * WINDOW + 2 :]
    blocks, bores, tile = other[0].shape
    blocks -= 1
    me = lax.axis_index("rows")
    chip, core = me // 2, lax.rem(me, 2)
    seg_rows = heat_mine.shape[0]
    offsets = (0,) + hop_offsets(chip)
    for pieces, side in ((mine, core), (other, 1 - core)):
        for piece, offset in zip(pieces, offsets):
            at = pl.multiple_of((offset + CHIP_REACH) * 2 * bores + side * bores, bores)
            scale = jnp.exp2(block_of(piece, blocks, tile) - CODE_BITS)
            for block in range(blocks):
                top, rest_of = split(block_of(piece, block, tile) * scale)
                high[pl.ds(at, bores), block * tile : (block + 1) * tile] = top
                low[pl.ds(at, bores), block * tile : (block + 1) * tile] = rest_of
    heat[pl.ds(pl.multiple_of(core * seg_rows, seg_rows), seg_rows)] = heat_mine[...]
    heat[pl.ds(pl.multiple_of((1 - core) * seg_rows, seg_rows), seg_rows)] = heat_other[...]
    for slot in range(WINDOW):
        at = pl.multiple_of(slot * 2 * bores + core * bores, bores)
        left[slot * bores : (slot + 1) * bores] = high[pl.ds(at, bores)]
        left[(WINDOW + slot) * bores : (WINDOW + slot + 1) * bores] = low[pl.ds(at, bores)]
    rows = WINDOW * bores
    transposed = (((1,), (1,)), ((), ()))
    both = lax.dot_general(left[...], high[...], transposed, preferred_element_type=F32)
    cross = lax.dot_general(left[:rows], low[...], transposed, preferred_element_type=F32)
    gram = both[:rows] + both[rows:] + cross
    warm = jnp.dot(left[...], heat[...], preferred_element_type=F32)
    warm = warm[:rows] + warm[rows:]
    span = 2 * bores
    width = 3 * 2 * span
    lane = lax.broadcasted_iota(jnp.int32, (bores, width), 1)
    padded = jnp.concatenate(
        [gram, jnp.zeros((rows, width - WINDOW * span), F32)], axis=1
    )
    for slot in range(WINDOW):
        offset = slot - CHIP_REACH
        base = padded[slot * bores : (slot + 1) * bores]
        odd = lax.rem(chip + offset + 2, 2)
        places = []
        for parity in (0, 1):
            shift = (CHIP_REACH - offset + parity) * span
            moved = pltpu.roll(base, shift % width, 1) if shift % width else base
            keep = (lane >= shift) & (lane < (WINDOW + parity) * span)
            places.append(jnp.where(keep, moved, 0.0))
        shifted[slot, :, :width] = jnp.where(odd == 1, places[1], places[0])
        shifted[slot, :, width:] = warm[slot * bores : (slot + 1) * bores]
    _, counts = bounds(lengths_ref[...], bores)
    odd = lax.rem(chip, 2)
    free = ((odd == 1) & (lane < span)) | ((odd == 0) & (lane >= WINDOW * span))
    shifted[CHIP_REACH, :, :width] = jnp.where(
        free, counts, shifted[CHIP_REACH, :, :width]
    )
    shifted[CHIP_REACH, :, width:] = (
        shifted[CHIP_REACH, :, width:] - counts * recorded_ref[...]
    )
    for out, offset in zip(outs, offsets):
        out[...] = shifted[offset + CHIP_REACH]


def transpose_kernel(*rest):
    mine, other = rest[:WINDOW], rest[WINDOW : 2 * WINDOW]
    high, low = rest[2 * WINDOW : 2 * WINDOW + 2]
    (rows_of,) = rest[2 * WINDOW + 2 :]
    blocks, bores, tile = other[0].shape
    blocks -= 1
    own_blocks = blocks // 2
    me = lax.axis_index("rows")
    chip, core = me // 2, lax.rem(me, 2)
    for pieces, side in ((mine, core), (other, 1 - core)):
        for piece, offset in zip(pieces, (0,) + hop_offsets(chip)):
            at = pl.multiple_of((offset + CHIP_REACH) * 2 * bores + side * bores, bores)
            scale = jnp.exp2(block_of(piece, blocks, tile) - CODE_BITS)
            for block in range(own_blocks):
                rows_of[block, pl.ds(at, bores)] = scale * block_of(
                    piece, core * own_blocks + block, tile
                )
    for block in range(own_blocks):
        top, rest_of = split(rows_of[block].T)
        high[block * tile : (block + 1) * tile] = top
        low[block * tile : (block + 1) * tile] = rest_of


def descend_kernel(ranks, places, heat_hbm, high_ref, low_ref, *rest):
    pieces, rest = rest[: len(places)], rest[len(places) :]
    heat_out, misfit_out = rest[:2]
    lower, band, counts, misfit, warm, shares, heat_ref, heat_sem = rest[2:]
    fetch = pltpu.make_async_copy(heat_hbm, heat_ref, heat_sem)
    fetch.start()
    bores, columns = misfit_out.shape
    width = lower.shape[1]
    plane = 4 * bores
    planes = ranks // 4
    span = 2 * bores
    me = lax.axis_index("rows")
    lane = lax.broadcasted_iota(jnp.int32, (bores, width), 1)
    for indices, piece in zip(places, pieces):
        for part, index in enumerate(indices):
            here = slice(part * bores, (part + 1) * bores)
            rank = jnp.bitwise_xor(me, index)
            at = pl.multiple_of(rank * bores, bores)
            odd = lax.rem(rank // 2, 2) == 1
            count = jnp.where(odd, piece[here, :1], piece[here, width - 1 : width])
            free = (odd & (lane < span)) | (
                jnp.logical_not(odd) & (lane >= WINDOW * span)
            )
            lower[pl.ds(at, bores)] = jnp.where(free, 0.0, piece[here, :width])
            misfit[pl.ds(at, bores)] = piece[here, width:] / count
            counts[pl.ds(at, bores)] = jnp.broadcast_to(count, (bores, columns))
    half_row = lax.broadcasted_iota(jnp.int32, (plane, plane), 0) < span
    half_col = lax.broadcasted_iota(jnp.int32, (plane, plane), 1) >= span
    for p in range(planes):
        rows = lower[p * plane : (p + 1) * plane]
        diagonal = rows[:, 2 * plane :]
        diagonal = jnp.where(half_row & half_col, diagonal.T, diagonal)
        whole = {0: diagonal}
        for step in (1, 2):
            if p - step >= 0:
                whole[-step] = rows[:, (2 - step) * plane : (3 - step) * plane]
            if p + step < planes:
                following = lower[(p + step) * plane : (p + step + 1) * plane]
                whole[step] = following[:, (2 - step) * plane : (3 - step) * plane].T
        for step, part in whole.items():
            top, rest_of = split(part)
            at = (step + 2) * plane
            band[p, :plane, at : at + plane] = top
            band[p, plane:, at : at + plane] = rest_of
    shares[: 2 * plane] = jnp.zeros((2 * plane, ITERS * columns), BF16)
    shares[(planes + 2) * plane :] = jnp.zeros((2 * plane, ITERS * columns), BF16)
    first = pl.multiple_of((me // 2 - CHIP_REACH) * span + 2 * plane, span)
    steps = []
    for iteration in range(ITERS):
        lanes = slice(iteration * columns, (iteration + 1) * columns)
        shares[2 * plane : (planes + 2) * plane, lanes] = (
            misfit[...] / counts[...]
        ).astype(BF16)
        if iteration == ITERS - 1:
            near = shares[pl.ds(first, WINDOW * span)]
            gradients = jnp.dot(
                high_ref[...], near, preferred_element_type=F32
            ) + jnp.dot(low_ref[...], near, preferred_element_type=F32)
        power = jnp.zeros((plane, columns), F32)
        curvature = jnp.zeros((plane, columns), F32)
        for p in range(planes):
            start, stop = max(p - 2, 0), min(p + 3, planes)
            both = jnp.dot(
                band[p, :, (start - p + 2) * plane : (stop - p + 2) * plane],
                shares[(start + 2) * plane : (stop + 2) * plane, lanes],
                preferred_element_type=F32,
            )
            swept = both[:plane] + both[plane:]
            here = shares[(p + 2) * plane : (p + 3) * plane, lanes].astype(F32)
            image = swept / counts[p * plane : (p + 1) * plane]
            warm[p * plane : (p + 1) * plane] = image
            power = power + here * swept
            curvature = curvature + image * image
        step = jnp.sum(power) / (jnp.sum(curvature) + 1e-06)
        steps.append(step)
        if iteration < ITERS - 1:
            misfit[...] = misfit[...] - step * warm[...]
    mine = pl.ds(pl.multiple_of(me * bores, bores), bores)
    misfit_out[...] = misfit[mine] - steps[-1] * warm[mine]
    fetch.wait()
    heat = heat_ref[...]
    for iteration in range(ITERS):
        heat = heat - steps[iteration] * gradients[
            :, iteration * columns : (iteration + 1) * columns
        ]
    heat_out[...] = heat


def on_device(
    ranks, response_tiles, tile_cols, tile_count, heat_start, recorded, bore_lengths
):
    block_rows, slots, tile = response_tiles.shape[:3]
    seg_rows, columns = heat_start.shape
    bores = bore_lengths.shape[1]
    per_chip = 2 * block_rows
    rows = WINDOW * bores
    span = 2 * bores
    width = 6 * span
    hops = hop_pairs(ranks)
    limit = pltpu.CompilerParams(vmem_limit_bytes=48 << 20)

    def send(value, pairs):
        return lax.ppermute(value, "rows", pairs)

    def swap(value, bit):
        return send(value, [(rank, rank ^ bit) for rank in range(ranks)])

    piece = jax.ShapeDtypeStruct((per_chip + 1, bores, tile), I16)
    sent = pl.pallas_call(
        compress_kernel,
        out_shape=(piece,) * WINDOW,
        in_specs=[HBM] * 4,
        out_specs=(VMEM,) * WINDOW,
        scratch_shapes=[
            pltpu.SMEM(tile_cols.shape, jnp.int32),
            pltpu.SMEM(tile_count.shape, jnp.int32),
            pltpu.VMEM(bore_lengths.shape, jnp.int32),
            pltpu.VMEM((WINDOW * per_chip + 1, bores, tile), F32),
            pltpu.VMEM((block_rows, slots, tile, tile), BF16),
            pltpu.SemaphoreType.DMA((3,)),
            pltpu.SemaphoreType.DMA((block_rows,)),
        ],
        compiler_params=pltpu.CompilerParams(vmem_limit_bytes=60 << 20),
        name="compress",
    )(tile_cols, tile_count, bore_lengths, response_tiles)
    mine = [sent[0]] + [send(value, pairs) for value, pairs in zip(sent[1:], hops)]
    mine[1], heat_late, own = lax.optimization_barrier((mine[1], heat_start, mine[0]))
    heat_low = heat_late.astype(BF16)
    heat_other = swap(heat_low, 1)
    own = own.transpose(1, 0, 2).reshape(bores, (per_chip + 1) * tile)
    mine[2], own = lax.optimization_barrier((mine[2], own))
    other = [swap(value, 1) for value in mine]
    mine[0] = own
    packed = jax.ShapeDtypeStruct((bores, width + columns), F32)
    partial = pl.pallas_call(
        gram_kernel,
        out_shape=(packed,) * WINDOW,
        in_specs=[VMEM] * (2 * WINDOW + 4),
        out_specs=(VMEM,) * WINDOW,
        scratch_shapes=[
            pltpu.VMEM((WINDOW * span, per_chip * tile), BF16),
            pltpu.VMEM((WINDOW * span, per_chip * tile), BF16),
            pltpu.VMEM((2 * seg_rows, columns), BF16),
            pltpu.VMEM((2 * rows, per_chip * tile), BF16),
            pltpu.VMEM((WINDOW, bores, width + columns), F32),
        ],
        compiler_params=limit,
        name="gram",
    )(bore_lengths, recorded, *mine, *other, heat_low, heat_other)
    parts = [partial[0]] + [send(value, pairs) for value, pairs in zip(partial[1:], hops)]
    turned = jax.ShapeDtypeStruct((seg_rows, WINDOW * span), BF16)
    high, low = pl.pallas_call(
        transpose_kernel,
        out_shape=(turned, turned),
        in_specs=[VMEM] * (2 * WINDOW),
        out_specs=(VMEM, VMEM),
        scratch_shapes=[pltpu.VMEM((block_rows, WINDOW * span, tile), F32)],
        compiler_params=limit,
        name="turn",
    )(*mine, *other)
    total, high, low = lax.optimization_barrier((parts[0], high, low))
    for part in parts[1:]:
        total = total + part
    column = {0: total}
    for index in (8, 4, 12):
        if index < ranks:
            column[index] = swap(total, index)
    bit = 16
    while bit < ranks:
        column.update({index ^ bit: swap(value, bit) for index, value in list(column.items())})
        bit *= 2
    beside = {index: swap(value, 2) for index, value in column.items()}
    across = {
        index: swap(jnp.concatenate([value, beside[index]], axis=0), 1)
        for index, value in column.items()
    }
    places = tuple(
        [(index,) for index in column]
        + [(index ^ 2,) for index in column]
        + [(index ^ 1, index ^ 3) for index in column]
    )
    gathered = list(column.values()) + list(beside.values()) + list(across.values())
    return pl.pallas_call(
        functools.partial(descend_kernel, ranks, places),
        out_shape=(
            jax.ShapeDtypeStruct((seg_rows, columns), F32),
            jax.ShapeDtypeStruct((bores, columns), F32),
        ),
        in_specs=[HBM] + [VMEM] * (2 + len(gathered)),
        out_specs=(VMEM, VMEM),
        scratch_shapes=[
            pltpu.VMEM((ranks * bores, width), F32),
            pltpu.VMEM((ranks // 4, 8 * bores, 20 * bores), BF16),
            pltpu.VMEM((ranks * bores, columns), F32),
            pltpu.VMEM((ranks * bores, columns), F32),
            pltpu.VMEM((ranks * bores, columns), F32),
            pltpu.VMEM(((ranks + 16) * bores, ITERS * columns), BF16),
            pltpu.VMEM((seg_rows, columns), F32),
            pltpu.SemaphoreType.DMA,
        ],
        compiler_params=limit,
        name="descend",
    )(heat_start, high, low, *gathered)


def solution(mesh):
    placed = (
        P(("groups", "rows"), None, None, None),
        P(("groups", "rows"), None),
        P(("groups", "rows")),
        P(("groups", "rows"), None),
        P(("groups", "rows"), None),
        P(("groups", "rows"), None),
    )
    return jax.shard_map(
        functools.partial(on_device, mesh.shape["rows"]),
        mesh=mesh,
        in_specs=placed,
        out_specs=(P(("groups", "rows"), None), P(("groups", "rows"), None)),
        check_vma=False,
    )
```

```python
import functools

import jax
import jax.numpy as jnp
from jax import lax
from jax.experimental import pallas as pl
from jax.experimental.pallas import tpu as pltpu
from jax.sharding import PartitionSpec as P

REACH = 4
ITERS = 2
CHIP_REACH = REACH // 2
WINDOW = 2 * CHIP_REACH + 1
F32 = jnp.float32
BF16 = jnp.bfloat16
I16 = jnp.int16
CODE_BITS = 15.0
CODE_MOST = 32767.0
VMEM = pl.BlockSpec(memory_space=pltpu.VMEM)
HBM = pl.BlockSpec(memory_space=pltpu.HBM)


def hop_offsets(chip):
    near = 1 - 2 * lax.rem(chip, 2)
    far = 2 - 4 * lax.rem(chip // 2, 2)
    return (-near, -far, far, near)


def hop_pairs(ranks):
    chips = ranks // 2
    groups = []
    for step, phase in ((1, 1), (2, 1), (2, 0), (1, 0)):
        pairs = []
        for chip in range(chips - step):
            if (chip // step) % 2 == phase:
                for core in (0, 1):
                    low, high = 2 * chip + core, 2 * (chip + step) + core
                    pairs += [(low, high), (high, low)]
        busy = {source for source, _ in pairs}
        pairs += [(rank, rank ^ 1) for rank in range(ranks) if rank not in busy]
        groups.append(pairs)
    return groups


def bounds(lengths, bores):
    upto = lax.broadcasted_iota(jnp.int32, (bores, bores), 1) <= lax.broadcasted_iota(
        jnp.int32, (bores, bores), 0
    )
    ends = jnp.sum(jnp.where(upto, lengths.astype(F32), 0.0), axis=1, keepdims=True)
    here = lax.broadcasted_iota(jnp.int32, (bores, bores), 1) == lax.broadcasted_iota(
        jnp.int32, (bores, bores), 0
    )
    counts = jnp.sum(jnp.where(here, lengths.astype(F32), 0.0), axis=1, keepdims=True)
    return ends, counts


def compress_kernel(cols_hbm, count_hbm, lengths_hbm, tiles_hbm, *rest):
    outs = rest[: WINDOW]
    cols_ref, count_ref, lengths_ref, slab, tiles, small_sems, sems = rest[WINDOW:]
    small = []
    for index, (source, target) in enumerate(
        ((cols_hbm, cols_ref), (count_hbm, count_ref), (lengths_hbm, lengths_ref))
    ):
        copy = pltpu.make_async_copy(source, target, small_sems.at[index])
        copy.start()
        small.append(copy)
    block_rows, slots, tile = tiles.shape[0], tiles.shape[1], tiles.shape[2]
    bores = slab.shape[1]
    per_chip = 2 * block_rows
    copies = []
    for row in range(block_rows):
        copy = pltpu.make_async_copy(tiles_hbm.at[row], tiles.at[row], sems.at[row])
        copy.start(priority=row // 2)
        copies.append(copy)
    slab[...] = jnp.zeros_like(slab)
    chip = lax.axis_index("rows") // 2
    for copy in small:
        copy.wait()
    first_block = (chip - CHIP_REACH) * per_chip
    ends, counts = bounds(lengths_ref[...], bores)
    starts = ends - counts
    members = []
    for row in range(block_rows):
        position = (
            lax.broadcasted_iota(jnp.int32, (bores, tile), 1) + row * tile
        ).astype(F32)
        inside = (position >= starts) & (position < ends)
        members.append(inside.astype(F32).astype(BF16))
    empty = jnp.zeros((bores, tile), BF16)
    for row in range(0, block_rows, 2):
        upper = jnp.concatenate([members[row], empty], axis=1)
        under = jnp.concatenate([empty, members[row + 1]], axis=1)
        left = jnp.concatenate([upper, under], axis=0)
        copies[row].wait()
        copies[row + 1].wait()
        for slot in range(0, slots, 2):
            right = jnp.concatenate(
                [
                    jnp.concatenate([tiles[at, slot], tiles[at, slot + 1]], axis=1)
                    for at in (row, row + 1)
                ],
                axis=0,
            )
            product = jnp.dot(left, right, preferred_element_type=F32)
            for i in range(2):
                for j in range(2):
                    place = jnp.where(
                        slot + j < count_ref[row + i],
                        cols_ref[row + i, slot + j] - first_block,
                        WINDOW * per_chip,
                    )
                    slab[place] += product[
                        i * bores : (i + 1) * bores, j * tile : (j + 1) * tile
                    ]
    largest = jnp.max(jnp.abs(slab[: WINDOW * per_chip]), axis=0)
    largest = jnp.max(largest, axis=1, keepdims=True)
    exponent = jnp.ceil(jnp.log2(jnp.maximum(largest, 1e-30)))
    scale = jnp.broadcast_to(jnp.exp2(CODE_BITS - exponent), (bores, tile))
    exponent = jnp.broadcast_to(exponent, (bores, tile)).astype(jnp.int32).astype(I16)
    for out, offset in zip(outs, (0,) + hop_offsets(chip)):
        for block in range(per_chip):
            value = slab[(offset + CHIP_REACH) * per_chip + block]
            code = jnp.minimum(jnp.round(value * scale), CODE_MOST)
            out[block] = code.astype(jnp.int32).astype(I16)
        out[per_chip] = exponent


def split(value):
    high = value.astype(BF16)
    return high, (value - high.astype(F32)).astype(BF16)


def block_of(piece, block, tile):
    if len(piece.shape) == 3:
        code = piece[block]
    else:
        code = piece[:, pl.ds(pl.multiple_of(block * tile, tile), tile)]
    return code.astype(jnp.int32).astype(F32)


def gram_kernel(lengths_ref, recorded_ref, *rest):
    mine, other = rest[:WINDOW], rest[WINDOW : 2 * WINDOW]
    heat_mine, heat_other = rest[2 * WINDOW : 2 * WINDOW + 2]
    outs = rest[2 * WINDOW + 2 : 3 * WINDOW + 2]
    high, low, heat, left, shifted = rest[3 * WINDOW + 2 :]
    blocks, bores, tile = other[0].shape
    blocks -= 1
    me = lax.axis_index("rows")
    chip, core = me // 2, lax.rem(me, 2)
    seg_rows = heat_mine.shape[0]
    offsets = (0,) + hop_offsets(chip)
    for pieces, side in ((mine, core), (other, 1 - core)):
        for piece, offset in zip(pieces, offsets):
            at = pl.multiple_of((offset + CHIP_REACH) * 2 * bores + side * bores, bores)
            scale = jnp.exp2(block_of(piece, blocks, tile) - CODE_BITS)
            for block in range(blocks):
                top, rest_of = split(block_of(piece, block, tile) * scale)
                high[pl.ds(at, bores), block * tile : (block + 1) * tile] = top
                low[pl.ds(at, bores), block * tile : (block + 1) * tile] = rest_of
    heat[pl.ds(pl.multiple_of(core * seg_rows, seg_rows), seg_rows)] = heat_mine[...]
    heat[pl.ds(pl.multiple_of((1 - core) * seg_rows, seg_rows), seg_rows)] = heat_other[...]
    for slot in range(WINDOW):
        at = pl.multiple_of(slot * 2 * bores + core * bores, bores)
        left[slot * bores : (slot + 1) * bores] = high[pl.ds(at, bores)]
        left[(WINDOW + slot) * bores : (WINDOW + slot + 1) * bores] = low[pl.ds(at, bores)]
    rows = WINDOW * bores
    transposed = (((1,), (1,)), ((), ()))
    both = lax.dot_general(left[...], high[...], transposed, preferred_element_type=F32)
    cross = lax.dot_general(left[:rows], low[...], transposed, preferred_element_type=F32)
    gram = both[:rows] + both[rows:] + cross
    warm = jnp.dot(left[...], heat[...], preferred_element_type=F32)
    warm = warm[:rows] + warm[rows:]
    span = 2 * bores
    width = 3 * 2 * span
    lane = lax.broadcasted_iota(jnp.int32, (bores, width), 1)
    padded = jnp.concatenate(
        [gram, jnp.zeros((rows, width - WINDOW * span), F32)], axis=1
    )
    for slot in range(WINDOW):
        offset = slot - CHIP_REACH
        base = padded[slot * bores : (slot + 1) * bores]
        odd = lax.rem(chip + offset + 2, 2)
        places = []
        for parity in (0, 1):
            shift = (CHIP_REACH - offset + parity) * span
            moved = pltpu.roll(base, shift % width, 1) if shift % width else base
            keep = (lane >= shift) & (lane < (WINDOW + parity) * span)
            places.append(jnp.where(keep, moved, 0.0))
        shifted[slot, :, :width] = jnp.where(odd == 1, places[1], places[0])
        shifted[slot, :, width:] = warm[slot * bores : (slot + 1) * bores]
    _, counts = bounds(lengths_ref[...], bores)
    odd = lax.rem(chip, 2)
    free = ((odd == 1) & (lane < span)) | ((odd == 0) & (lane >= WINDOW * span))
    shifted[CHIP_REACH, :, :width] = jnp.where(
        free, counts, shifted[CHIP_REACH, :, :width]
    )
    shifted[CHIP_REACH, :, width:] = (
        shifted[CHIP_REACH, :, width:] - counts * recorded_ref[...]
    )
    for out, offset in zip(outs, offsets):
        out[...] = shifted[offset + CHIP_REACH]


def transpose_kernel(*rest):
    mine, other = rest[:WINDOW], rest[WINDOW : 2 * WINDOW]
    high, low = rest[2 * WINDOW : 2 * WINDOW + 2]
    (rows_of,) = rest[2 * WINDOW + 2 :]
    blocks, bores, tile = other[0].shape
    blocks -= 1
    own_blocks = blocks // 2
    me = lax.axis_index("rows")
    chip, core = me // 2, lax.rem(me, 2)
    for pieces, side in ((mine, core), (other, 1 - core)):
        for piece, offset in zip(pieces, (0,) + hop_offsets(chip)):
            at = pl.multiple_of((offset + CHIP_REACH) * 2 * bores + side * bores, bores)
            scale = jnp.exp2(block_of(piece, blocks, tile) - CODE_BITS)
            for block in range(own_blocks):
                rows_of[block, pl.ds(at, bores)] = scale * block_of(
                    piece, core * own_blocks + block, tile
                )
    for block in range(own_blocks):
        top, rest_of = split(rows_of[block].T)
        high[block * tile : (block + 1) * tile] = top
        low[block * tile : (block + 1) * tile] = rest_of


def descend_kernel(ranks, places, heat_hbm, high_ref, low_ref, *rest):
    pieces, rest = rest[: len(places)], rest[len(places) :]
    heat_out, misfit_out = rest[:2]
    lower, band, counts, misfit, warm, shares, heat_ref, heat_sem = rest[2:]
    fetch = pltpu.make_async_copy(heat_hbm, heat_ref, heat_sem)
    fetch.start()
    bores, columns = misfit_out.shape
    width = lower.shape[1]
    plane = 4 * bores
    planes = ranks // 4
    span = 2 * bores
    me = lax.axis_index("rows")
    lane = lax.broadcasted_iota(jnp.int32, (bores, width), 1)
    for indices, piece in zip(places, pieces):
        for part, index in enumerate(indices):
            here = slice(part * bores, (part + 1) * bores)
            rank = jnp.bitwise_xor(me, index)
            at = pl.multiple_of(rank * bores, bores)
            odd = lax.rem(rank // 2, 2) == 1
            count = jnp.where(odd, piece[here, :1], piece[here, width - 1 : width])
            free = (odd & (lane < span)) | (
                jnp.logical_not(odd) & (lane >= WINDOW * span)
            )
            lower[pl.ds(at, bores)] = jnp.where(free, 0.0, piece[here, :width])
            misfit[pl.ds(at, bores)] = piece[here, width:] / count
            counts[pl.ds(at, bores)] = jnp.broadcast_to(count, (bores, columns))
    half_row = lax.broadcasted_iota(jnp.int32, (plane, plane), 0) < span
    half_col = lax.broadcasted_iota(jnp.int32, (plane, plane), 1) >= span
    for p in range(planes):
        rows = lower[p * plane : (p + 1) * plane]
        diagonal = rows[:, 2 * plane :]
        diagonal = jnp.where(half_row & half_col, diagonal.T, diagonal)
        whole = {0: diagonal}
        for step in (1, 2):
            if p - step >= 0:
                whole[-step] = rows[:, (2 - step) * plane : (3 - step) * plane]
            if p + step < planes:
                following = lower[(p + step) * plane : (p + step + 1) * plane]
                whole[step] = following[:, (2 - step) * plane : (3 - step) * plane].T
        for step, part in whole.items():
            top, rest_of = split(part)
            at = (step + 2) * plane
            band[p, :plane, at : at + plane] = top
            band[p, plane:, at : at + plane] = rest_of
    shares[: 2 * plane] = jnp.zeros((2 * plane, ITERS * columns), BF16)
    shares[(planes + 2) * plane :] = jnp.zeros((2 * plane, ITERS * columns), BF16)
    first = pl.multiple_of((me // 2 - CHIP_REACH) * span + 2 * plane, span)
    steps = []
    for iteration in range(ITERS):
        lanes = slice(iteration * columns, (iteration + 1) * columns)
        shares[2 * plane : (planes + 2) * plane, lanes] = (
            misfit[...] / counts[...]
        ).astype(BF16)
        if iteration == ITERS - 1:
            near = shares[pl.ds(first, WINDOW * span)]
            gradients = jnp.dot(
                high_ref[...], near, preferred_element_type=F32
            ) + jnp.dot(low_ref[...], near, preferred_element_type=F32)
        power = jnp.zeros((plane, columns), F32)
        curvature = jnp.zeros((plane, columns), F32)
        for p in range(planes):
            start, stop = max(p - 2, 0), min(p + 3, planes)
            both = jnp.dot(
                band[p, :, (start - p + 2) * plane : (stop - p + 2) * plane],
                shares[(start + 2) * plane : (stop + 2) * plane, lanes],
                preferred_element_type=F32,
            )
            swept = both[:plane] + both[plane:]
            here = shares[(p + 2) * plane : (p + 3) * plane, lanes].astype(F32)
            image = swept / counts[p * plane : (p + 1) * plane]
            warm[p * plane : (p + 1) * plane] = image
            power = power + here * swept
            curvature = curvature + image * image
        step = jnp.sum(power) / (jnp.sum(curvature) + 1e-06)
        steps.append(step)
        if iteration < ITERS - 1:
            misfit[...] = misfit[...] - step * warm[...]
    mine = pl.ds(pl.multiple_of(me * bores, bores), bores)
    misfit_out[...] = misfit[mine] - steps[-1] * warm[mine]
    fetch.wait()
    heat = heat_ref[...]
    for iteration in range(ITERS):
        heat = heat - steps[iteration] * gradients[
            :, iteration * columns : (iteration + 1) * columns
        ]
    heat_out[...] = heat


def on_device(
    ranks, response_tiles, tile_cols, tile_count, heat_start, recorded, bore_lengths
):
    block_rows, slots, tile = response_tiles.shape[:3]
    seg_rows, columns = heat_start.shape
    bores = bore_lengths.shape[1]
    per_chip = 2 * block_rows
    rows = WINDOW * bores
    span = 2 * bores
    width = 6 * span
    hops = hop_pairs(ranks)
    limit = pltpu.CompilerParams(vmem_limit_bytes=48 << 20)

    def send(value, pairs):
        return lax.ppermute(value, "rows", pairs)

    def swap(value, bit):
        return send(value, [(rank, rank ^ bit) for rank in range(ranks)])

    piece = jax.ShapeDtypeStruct((per_chip + 1, bores, tile), I16)
    sent = pl.pallas_call(
        compress_kernel,
        out_shape=(piece,) * WINDOW,
        in_specs=[HBM] * 4,
        out_specs=(VMEM,) * WINDOW,
        scratch_shapes=[
            pltpu.SMEM(tile_cols.shape, jnp.int32),
            pltpu.SMEM(tile_count.shape, jnp.int32),
            pltpu.VMEM(bore_lengths.shape, jnp.int32),
            pltpu.VMEM((WINDOW * per_chip + 1, bores, tile), F32),
            pltpu.VMEM((block_rows, slots, tile, tile), BF16),
            pltpu.SemaphoreType.DMA((3,)),
            pltpu.SemaphoreType.DMA((block_rows,)),
        ],
        compiler_params=pltpu.CompilerParams(vmem_limit_bytes=60 << 20),
        name="compress",
    )(tile_cols, tile_count, bore_lengths, response_tiles)
    mine = [sent[0]] + [send(value, pairs) for value, pairs in zip(sent[1:], hops)]
    mine[1], heat_late, own = lax.optimization_barrier((mine[1], heat_start, mine[0]))
    heat_low = heat_late.astype(BF16)
    heat_other = swap(heat_low, 1)
    own = own.transpose(1, 0, 2).reshape(bores, (per_chip + 1) * tile)
    mine[2], own = lax.optimization_barrier((mine[2], own))
    other = [swap(value, 1) for value in mine]
    mine[0] = own
    packed = jax.ShapeDtypeStruct((bores, width + columns), F32)
    partial = pl.pallas_call(
        gram_kernel,
        out_shape=(packed,) * WINDOW,
        in_specs=[VMEM] * (2 * WINDOW + 4),
        out_specs=(VMEM,) * WINDOW,
        scratch_shapes=[
            pltpu.VMEM((WINDOW * span, per_chip * tile), BF16),
            pltpu.VMEM((WINDOW * span, per_chip * tile), BF16),
            pltpu.VMEM((2 * seg_rows, columns), BF16),
            pltpu.VMEM((2 * rows, per_chip * tile), BF16),
            pltpu.VMEM((WINDOW, bores, width + columns), F32),
        ],
        compiler_params=limit,
        name="gram",
    )(bore_lengths, recorded, *mine, *other, heat_low, heat_other)
    parts = [partial[0]] + [send(value, pairs) for value, pairs in zip(partial[1:], hops)]
    turned = jax.ShapeDtypeStruct((seg_rows, WINDOW * span), BF16)
    high, low = pl.pallas_call(
        transpose_kernel,
        out_shape=(turned, turned),
        in_specs=[VMEM] * (2 * WINDOW),
        out_specs=(VMEM, VMEM),
        scratch_shapes=[pltpu.VMEM((block_rows, WINDOW * span, tile), F32)],
        compiler_params=limit,
        name="turn",
    )(*mine, *other)
    total, high, low = lax.optimization_barrier((parts[0], high, low))
    for part in parts[1:]:
        total = total + part
    column = {0: total}
    for index in (8, 4, 12):
        if index < ranks:
            column[index] = swap(total, index)
    bit = 16
    while bit < ranks:
        column.update({index ^ bit: swap(value, bit) for index, value in list(column.items())})
        bit *= 2
    beside = {index: swap(value, 2) for index, value in column.items()}
    across = {
        index: swap(jnp.concatenate([value, beside[index]], axis=0), 1)
        for index, value in column.items()
    }
    places = tuple(
        [(index,) for index in column]
        + [(index ^ 2,) for index in column]
        + [(index ^ 1, index ^ 3) for index in column]
    )
    gathered = list(column.values()) + list(beside.values()) + list(across.values())
    return pl.pallas_call(
        functools.partial(descend_kernel, ranks, places),
        out_shape=(
            jax.ShapeDtypeStruct((seg_rows, columns), F32),
            jax.ShapeDtypeStruct((bores, columns), F32),
        ),
        in_specs=[HBM] + [VMEM] * (2 + len(gathered)),
        out_specs=(VMEM, VMEM),
        scratch_shapes=[
            pltpu.VMEM((ranks * bores, width), F32),
            pltpu.VMEM((ranks // 4, 8 * bores, 20 * bores), BF16),
            pltpu.VMEM((ranks * bores, columns), F32),
            pltpu.VMEM((ranks * bores, columns), F32),
            pltpu.VMEM((ranks * bores, columns), F32),
            pltpu.VMEM(((ranks + 16) * bores, ITERS * columns), BF16),
            pltpu.VMEM((seg_rows, columns), F32),
            pltpu.SemaphoreType.DMA,
        ],
        compiler_params=limit,
        name="descend",
    )(heat_start, high, low, *gathered)


def solution(mesh):
    placed = (
        P(("groups", "rows"), None, None, None),
        P(("groups", "rows"), None),
        P(("groups", "rows")),
        P(("groups", "rows"), None),
        P(("groups", "rows"), None),
        P(("groups", "rows"), None),
    )
    return jax.shard_map(
        functools.partial(on_device, mesh.shape["rows"]),
        mesh=mesh,
        in_specs=placed,
        out_specs=(P(("groups", "rows"), None), P(("groups", "rows"), None)),
        check_vma=False,
    )
```

```python
import functools

import jax
import jax.numpy as jnp
from jax import lax
from jax.experimental import pallas as pl
from jax.experimental.pallas import tpu as pltpu
from jax.sharding import PartitionSpec as P

REACH = 4
ITERS = 2
CHIP_REACH = REACH // 2
WINDOW = 2 * CHIP_REACH + 1
F32 = jnp.float32
BF16 = jnp.bfloat16
I16 = jnp.int16
CODE_BITS = 15.0
CODE_MOST = 32767.0
VMEM = pl.BlockSpec(memory_space=pltpu.VMEM)
HBM = pl.BlockSpec(memory_space=pltpu.HBM)


def hop_offsets(chip):
    near = 1 - 2 * lax.rem(chip, 2)
    far = 2 - 4 * lax.rem(chip // 2, 2)
    return (-near, -far, far, near)


def hop_pairs(ranks):
    chips = ranks // 2
    groups = []
    for step, phase in ((1, 1), (2, 1), (2, 0), (1, 0)):
        pairs = []
        for chip in range(chips - step):
            if (chip // step) % 2 == phase:
                for core in (0, 1):
                    low, high = 2 * chip + core, 2 * (chip + step) + core
                    pairs += [(low, high), (high, low)]
        busy = {source for source, _ in pairs}
        pairs += [(rank, rank ^ 1) for rank in range(ranks) if rank not in busy]
        groups.append(pairs)
    return groups


def bounds(lengths, bores):
    upto = lax.broadcasted_iota(jnp.int32, (bores, bores), 1) <= lax.broadcasted_iota(
        jnp.int32, (bores, bores), 0
    )
    ends = jnp.sum(jnp.where(upto, lengths.astype(F32), 0.0), axis=1, keepdims=True)
    here = lax.broadcasted_iota(jnp.int32, (bores, bores), 1) == lax.broadcasted_iota(
        jnp.int32, (bores, bores), 0
    )
    counts = jnp.sum(jnp.where(here, lengths.astype(F32), 0.0), axis=1, keepdims=True)
    return ends, counts


def compress_kernel(cols_hbm, count_hbm, lengths_hbm, tiles_hbm, *rest):
    outs = rest[: WINDOW]
    cols_ref, count_ref, lengths_ref, slab, tiles, small_sems, sems = rest[WINDOW:]
    small = []
    for index, (source, target) in enumerate(
        ((cols_hbm, cols_ref), (count_hbm, count_ref), (lengths_hbm, lengths_ref))
    ):
        copy = pltpu.make_async_copy(source, target, small_sems.at[index])
        copy.start()
        small.append(copy)
    block_rows, slots, tile = tiles.shape[0], tiles.shape[1], tiles.shape[2]
    bores = slab.shape[1]
    per_chip = 2 * block_rows
    copies = []
    for row in range(block_rows):
        copy = pltpu.make_async_copy(tiles_hbm.at[row], tiles.at[row], sems.at[row])
        copy.start(priority=row // 2)
        copies.append(copy)
    slab[...] = jnp.zeros_like(slab)
    chip = lax.axis_index("rows") // 2
    for copy in small:
        copy.wait()
    first_block = (chip - CHIP_REACH) * per_chip
    ends, counts = bounds(lengths_ref[...], bores)
    starts = ends - counts
    members = []
    for row in range(block_rows):
        position = (
            lax.broadcasted_iota(jnp.int32, (bores, tile), 1) + row * tile
        ).astype(F32)
        inside = (position >= starts) & (position < ends)
        members.append(inside.astype(F32).astype(BF16))
    empty = jnp.zeros((bores, tile), BF16)
    for row in range(0, block_rows, 2):
        upper = jnp.concatenate([members[row], empty], axis=1)
        under = jnp.concatenate([empty, members[row + 1]], axis=1)
        left = jnp.concatenate([upper, under], axis=0)
        copies[row].wait()
        copies[row + 1].wait()
        for slot in range(0, slots, 2):
            right = jnp.concatenate(
                [
                    jnp.concatenate([tiles[at, slot], tiles[at, slot + 1]], axis=1)
                    for at in (row, row + 1)
                ],
                axis=0,
            )
            product = jnp.dot(left, right, preferred_element_type=F32)
            for i in range(2):
                for j in range(2):
                    place = jnp.where(
                        slot + j < count_ref[row + i],
                        cols_ref[row + i, slot + j] - first_block,
                        WINDOW * per_chip,
                    )
                    slab[place] += product[
                        i * bores : (i + 1) * bores, j * tile : (j + 1) * tile
                    ]
    largest = jnp.max(jnp.abs(slab[: WINDOW * per_chip]), axis=0)
    largest = jnp.max(largest, axis=1, keepdims=True)
    exponent = jnp.ceil(jnp.log2(jnp.maximum(largest, 1e-30)))
    scale = jnp.broadcast_to(jnp.exp2(CODE_BITS - exponent), (bores, tile))
    exponent = jnp.broadcast_to(exponent, (bores, tile)).astype(jnp.int32).astype(I16)
    for out, offset in zip(outs, (0,) + hop_offsets(chip)):
        for block in range(per_chip):
            value = slab[(offset + CHIP_REACH) * per_chip + block]
            code = jnp.minimum(jnp.round(value * scale), CODE_MOST)
            out[block] = code.astype(jnp.int32).astype(I16)
        out[per_chip] = exponent


def split(value):
    high = value.astype(BF16)
    return high, (value - high.astype(F32)).astype(BF16)


def block_of(piece, block, tile):
    if len(piece.shape) == 3:
        code = piece[block]
    else:
        code = piece[:, pl.ds(pl.multiple_of(block * tile, tile), tile)]
    return code.astype(jnp.int32).astype(F32)


def gram_kernel(lengths_ref, recorded_ref, *rest):
    mine, other = rest[:WINDOW], rest[WINDOW : 2 * WINDOW]
    heat_mine, heat_other = rest[2 * WINDOW : 2 * WINDOW + 2]
    outs = rest[2 * WINDOW + 2 : 3 * WINDOW + 2]
    high, low, heat, left, shifted = rest[3 * WINDOW + 2 :]
    blocks, bores, tile = other[0].shape
    blocks -= 1
    me = lax.axis_index("rows")
    chip, core = me // 2, lax.rem(me, 2)
    seg_rows = heat_mine.shape[0]
    offsets = (0,) + hop_offsets(chip)
    for pieces, side in ((mine, core), (other, 1 - core)):
        for piece, offset in zip(pieces, offsets):
            at = pl.multiple_of((offset + CHIP_REACH) * 2 * bores + side * bores, bores)
            scale = jnp.exp2(block_of(piece, blocks, tile) - CODE_BITS)
            for block in range(blocks):
                top, rest_of = split(block_of(piece, block, tile) * scale)
                high[pl.ds(at, bores), block * tile : (block + 1) * tile] = top
                low[pl.ds(at, bores), block * tile : (block + 1) * tile] = rest_of
    heat[pl.ds(pl.multiple_of(core * seg_rows, seg_rows), seg_rows)] = heat_mine[...]
    heat[pl.ds(pl.multiple_of((1 - core) * seg_rows, seg_rows), seg_rows)] = heat_other[...]
    for slot in range(WINDOW):
        at = pl.multiple_of(slot * 2 * bores + core * bores, bores)
        left[slot * bores : (slot + 1) * bores] = high[pl.ds(at, bores)]
        left[(WINDOW + slot) * bores : (WINDOW + slot + 1) * bores] = low[pl.ds(at, bores)]
    rows = WINDOW * bores
    transposed = (((1,), (1,)), ((), ()))
    both = lax.dot_general(left[...], high[...], transposed, preferred_element_type=F32)
    cross = lax.dot_general(left[:rows], low[...], transposed, preferred_element_type=F32)
    gram = both[:rows] + both[rows:] + cross
    warm = jnp.dot(left[...], heat[...], preferred_element_type=F32)
    warm = warm[:rows] + warm[rows:]
    span = 2 * bores
    width = 3 * 2 * span
    lane = lax.broadcasted_iota(jnp.int32, (bores, width), 1)
    padded = jnp.concatenate(
        [gram, jnp.zeros((rows, width - WINDOW * span), F32)], axis=1
    )
    for slot in range(WINDOW):
        offset = slot - CHIP_REACH
        base = padded[slot * bores : (slot + 1) * bores]
        parity = lax.rem(chip + offset + 2, 2)
        shift = (CHIP_REACH - offset + parity) * span
        keep = (lane >= shift) & (lane < (WINDOW + parity) * span)
        shifted[slot, :, :width] = jnp.where(keep, pltpu.roll(base, shift, 1), 0.0)
        shifted[slot, :, width:] = warm[slot * bores : (slot + 1) * bores]
    _, counts = bounds(lengths_ref[...], bores)
    odd = lax.rem(chip, 2)
    free = ((odd == 1) & (lane < span)) | ((odd == 0) & (lane >= WINDOW * span))
    shifted[CHIP_REACH, :, :width] = jnp.where(
        free, counts, shifted[CHIP_REACH, :, :width]
    )
    shifted[CHIP_REACH, :, width:] = (
        shifted[CHIP_REACH, :, width:] - counts * recorded_ref[...]
    )
    for out, offset in zip(outs, offsets):
        out[...] = shifted[offset + CHIP_REACH]


def transpose_kernel(*rest):
    mine, other = rest[:WINDOW], rest[WINDOW : 2 * WINDOW]
    high, low = rest[2 * WINDOW : 2 * WINDOW + 2]
    (rows_of,) = rest[2 * WINDOW + 2 :]
    blocks, bores, tile = other[0].shape
    blocks -= 1
    own_blocks = blocks // 2
    me = lax.axis_index("rows")
    chip, core = me // 2, lax.rem(me, 2)
    for pieces, side in ((mine, core), (other, 1 - core)):
        for piece, offset in zip(pieces, (0,) + hop_offsets(chip)):
            at = pl.multiple_of((offset + CHIP_REACH) * 2 * bores + side * bores, bores)
            scale = jnp.exp2(block_of(piece, blocks, tile) - CODE_BITS)
            for block in range(own_blocks):
                rows_of[block, pl.ds(at, bores)] = scale * block_of(
                    piece, core * own_blocks + block, tile
                )
    for block in range(own_blocks):
        top, rest_of = split(rows_of[block].T)
        high[block * tile : (block + 1) * tile] = top
        low[block * tile : (block + 1) * tile] = rest_of


def descend_kernel(ranks, places, heat_hbm, high_ref, low_ref, *rest):
    pieces, rest = rest[: len(places)], rest[len(places) :]
    heat_out, misfit_out = rest[:2]
    lower, band, counts, misfit, warm, shares, heat_ref, heat_sem = rest[2:]
    fetch = pltpu.make_async_copy(heat_hbm, heat_ref, heat_sem)
    fetch.start()
    bores, columns = misfit_out.shape
    width = lower.shape[1]
    plane = 4 * bores
    planes = ranks // 4
    span = 2 * bores
    me = lax.axis_index("rows")
    lane = lax.broadcasted_iota(jnp.int32, (bores, width), 1)
    for indices, piece in zip(places, pieces):
        for part, index in enumerate(indices):
            here = slice(part * bores, (part + 1) * bores)
            rank = jnp.bitwise_xor(me, index)
            at = pl.multiple_of(rank * bores, bores)
            odd = lax.rem(rank // 2, 2) == 1
            count = jnp.where(odd, piece[here, :1], piece[here, width - 1 : width])
            free = (odd & (lane < span)) | (
                jnp.logical_not(odd) & (lane >= WINDOW * span)
            )
            lower[pl.ds(at, bores)] = jnp.where(free, 0.0, piece[here, :width])
            misfit[pl.ds(at, bores)] = piece[here, width:] / count
            counts[pl.ds(at, bores)] = jnp.broadcast_to(count, (bores, columns))
    half_row = lax.broadcasted_iota(jnp.int32, (plane, plane), 0) < span
    half_col = lax.broadcasted_iota(jnp.int32, (plane, plane), 1) >= span
    for p in range(planes):
        rows = lower[p * plane : (p + 1) * plane]
        diagonal = rows[:, 2 * plane :]
        diagonal = jnp.where(half_row & half_col, diagonal.T, diagonal)
        whole = {0: diagonal}
        for step in (1, 2):
            if p - step >= 0:
                whole[-step] = rows[:, (2 - step) * plane : (3 - step) * plane]
            if p + step < planes:
                following = lower[(p + step) * plane : (p + step + 1) * plane]
                whole[step] = following[:, (2 - step) * plane : (3 - step) * plane].T
        for step, part in whole.items():
            top, rest_of = split(part)
            at = (step + 2) * plane
            band[p, :plane, at : at + plane] = top
            band[p, plane:, at : at + plane] = rest_of
    shares[: 2 * plane] = jnp.zeros((2 * plane, ITERS * columns), BF16)
    shares[(planes + 2) * plane :] = jnp.zeros((2 * plane, ITERS * columns), BF16)
    first = pl.multiple_of((me // 2 - CHIP_REACH) * span + 2 * plane, span)
    steps = []
    for iteration in range(ITERS):
        lanes = slice(iteration * columns, (iteration + 1) * columns)
        shares[2 * plane : (planes + 2) * plane, lanes] = (
            misfit[...] / counts[...]
        ).astype(BF16)
        if iteration == ITERS - 1:
            near = shares[pl.ds(first, WINDOW * span)]
            gradients = jnp.dot(
                high_ref[...], near, preferred_element_type=F32
            ) + jnp.dot(low_ref[...], near, preferred_element_type=F32)
        power = jnp.zeros((plane, columns), F32)
        curvature = jnp.zeros((plane, columns), F32)
        for p in range(planes):
            start, stop = max(p - 2, 0), min(p + 3, planes)
            both = jnp.dot(
                band[p, :, (start - p + 2) * plane : (stop - p + 2) * plane],
                shares[(start + 2) * plane : (stop + 2) * plane, lanes],
                preferred_element_type=F32,
            )
            swept = both[:plane] + both[plane:]
            here = shares[(p + 2) * plane : (p + 3) * plane, lanes].astype(F32)
            image = swept / counts[p * plane : (p + 1) * plane]
            warm[p * plane : (p + 1) * plane] = image
            power = power + here * swept
            curvature = curvature + image * image
        step = jnp.sum(power) / (jnp.sum(curvature) + 1e-06)
        steps.append(step)
        if iteration < ITERS - 1:
            misfit[...] = misfit[...] - step * warm[...]
    mine = pl.ds(pl.multiple_of(me * bores, bores), bores)
    misfit_out[...] = misfit[mine] - steps[-1] * warm[mine]
    fetch.wait()
    heat = heat_ref[...]
    for iteration in range(ITERS):
        heat = heat - steps[iteration] * gradients[
            :, iteration * columns : (iteration + 1) * columns
        ]
    heat_out[...] = heat


def on_device(
    ranks, response_tiles, tile_cols, tile_count, heat_start, recorded, bore_lengths
):
    block_rows, slots, tile = response_tiles.shape[:3]
    seg_rows, columns = heat_start.shape
    bores = bore_lengths.shape[1]
    per_chip = 2 * block_rows
    rows = WINDOW * bores
    span = 2 * bores
    width = 6 * span
    hops = hop_pairs(ranks)
    limit = pltpu.CompilerParams(vmem_limit_bytes=48 << 20)

    def send(value, pairs):
        return lax.ppermute(value, "rows", pairs)

    def swap(value, bit):
        return send(value, [(rank, rank ^ bit) for rank in range(ranks)])

    piece = jax.ShapeDtypeStruct((per_chip + 1, bores, tile), I16)
    sent = pl.pallas_call(
        compress_kernel,
        out_shape=(piece,) * WINDOW,
        in_specs=[HBM] * 4,
        out_specs=(VMEM,) * WINDOW,
        scratch_shapes=[
            pltpu.SMEM(tile_cols.shape, jnp.int32),
            pltpu.SMEM(tile_count.shape, jnp.int32),
            pltpu.VMEM(bore_lengths.shape, jnp.int32),
            pltpu.VMEM((WINDOW * per_chip + 1, bores, tile), F32),
            pltpu.VMEM((block_rows, slots, tile, tile), BF16),
            pltpu.SemaphoreType.DMA((3,)),
            pltpu.SemaphoreType.DMA((block_rows,)),
        ],
        compiler_params=pltpu.CompilerParams(vmem_limit_bytes=60 << 20),
        name="compress",
    )(tile_cols, tile_count, bore_lengths, response_tiles)
    mine = [sent[0]] + [send(value, pairs) for value, pairs in zip(sent[1:], hops)]
    mine[1], heat_late, own = lax.optimization_barrier((mine[1], heat_start, mine[0]))
    heat_low = heat_late.astype(BF16)
    heat_other = swap(heat_low, 1)
    own = own.transpose(1, 0, 2).reshape(bores, (per_chip + 1) * tile)
    mine[2], own = lax.optimization_barrier((mine[2], own))
    other = [swap(value, 1) for value in mine]
    mine[0] = own
    packed = jax.ShapeDtypeStruct((bores, width + columns), F32)
    partial = pl.pallas_call(
        gram_kernel,
        out_shape=(packed,) * WINDOW,
        in_specs=[VMEM] * (2 * WINDOW + 4),
        out_specs=(VMEM,) * WINDOW,
        scratch_shapes=[
            pltpu.VMEM((WINDOW * span, per_chip * tile), BF16),
            pltpu.VMEM((WINDOW * span, per_chip * tile), BF16),
            pltpu.VMEM((2 * seg_rows, columns), BF16),
            pltpu.VMEM((2 * rows, per_chip * tile), BF16),
            pltpu.VMEM((WINDOW, bores, width + columns), F32),
        ],
        compiler_params=limit,
        name="gram",
    )(bore_lengths, recorded, *mine, *other, heat_low, heat_other)
    parts = [partial[0]] + [send(value, pairs) for value, pairs in zip(partial[1:], hops)]
    turned = jax.ShapeDtypeStruct((seg_rows, WINDOW * span), BF16)
    high, low = pl.pallas_call(
        transpose_kernel,
        out_shape=(turned, turned),
        in_specs=[VMEM] * (2 * WINDOW),
        out_specs=(VMEM, VMEM),
        scratch_shapes=[pltpu.VMEM((block_rows, WINDOW * span, tile), F32)],
        compiler_params=limit,
        name="turn",
    )(*mine, *other)
    total, high, low = lax.optimization_barrier((parts[0], high, low))
    for part in parts[1:]:
        total = total + part
    column = {0: total}
    for index in (8, 4, 12):
        if index < ranks:
            column[index] = swap(total, index)
    bit = 16
    while bit < ranks:
        column.update({index ^ bit: swap(value, bit) for index, value in list(column.items())})
        bit *= 2
    beside = {index: swap(value, 2) for index, value in column.items()}
    across = {
        index: swap(jnp.concatenate([value, beside[index]], axis=0), 1)
        for index, value in column.items()
    }
    places = tuple(
        [(index,) for index in column]
        + [(index ^ 2,) for index in column]
        + [(index ^ 1, index ^ 3) for index in column]
    )
    gathered = list(column.values()) + list(beside.values()) + list(across.values())
    return pl.pallas_call(
        functools.partial(descend_kernel, ranks, places),
        out_shape=(
            jax.ShapeDtypeStruct((seg_rows, columns), F32),
            jax.ShapeDtypeStruct((bores, columns), F32),
        ),
        in_specs=[HBM] + [VMEM] * (2 + len(gathered)),
        out_specs=(VMEM, VMEM),
        scratch_shapes=[
            pltpu.VMEM((ranks * bores, width), F32),
            pltpu.VMEM((ranks // 4, 8 * bores, 20 * bores), BF16),
            pltpu.VMEM((ranks * bores, columns), F32),
            pltpu.VMEM((ranks * bores, columns), F32),
            pltpu.VMEM((ranks * bores, columns), F32),
            pltpu.VMEM(((ranks + 16) * bores, ITERS * columns), BF16),
            pltpu.VMEM((seg_rows, columns), F32),
            pltpu.SemaphoreType.DMA,
        ],
        compiler_params=limit,
        name="descend",
    )(heat_start, high, low, *gathered)


def solution(mesh):
    placed = (
        P(("groups", "rows"), None, None, None),
        P(("groups", "rows"), None),
        P(("groups", "rows")),
        P(("groups", "rows"), None),
        P(("groups", "rows"), None),
        P(("groups", "rows"), None),
    )
    return jax.shard_map(
        functools.partial(on_device, mesh.shape["rows"]),
        mesh=mesh,
        in_specs=placed,
        out_specs=(P(("groups", "rows"), None), P(("groups", "rows"), None)),
        check_vma=False,
    )
```
